128 devices in a mesh: row: 128 (over y, x, z, core).
Axes of the slice: x: 4, y: 4, z: 4, core: 2. Of those that a mesh axis runs over, the one named last changes fastest.
Arguments:
- displacement: float32 [512, 256, 2, 384], P('row'), may hold values from -6 to 6
- stiffness: bfloat16 [384, 384], replicated, may hold values from -0.3125 to 0.3125
- coupling: float32 [384], replicated, may hold values from 0.1 to 0.5
- softening: float32 [384], replicated, may hold values from 0.2 to 2
- electrode_mask: int32 [512, 256], P('row'), may hold values 0 or 1
- row_counts: int32 [128], replicated, may hold values from 1 to 4, 256 in all
- green_spectrum: float32 [4096, 4096], P('row'), may hold values from 0.25 to 1.25, as said below
Outputs:
- load_block: float32 [512, 256, 2, 384], P('row')
The draws below stay inside these ranges and needn't reach their ends.
Inputs may be any that keep to these rules, and one draw needn't show every extreme that they name: Device d holds row_counts[d] cell rows, following those of the devices before it; the entries sum to 256. `electrode_mask`: entries of unused slots are not read. green_spectrum equals its transpose, and green_spectrum[kx, ky] = green_spectrum[-kx mod 4096, ky] = green_spectrum[kx, -ky mod 4096].
All inputs are finite; a program needn't handle non-finite values. No bound on the sum of `electrode_mask` on one device may be relied on, other than what follows from the above.
Results may differ from the reference program's by a relative error of at most 0.0021.
Values sent between devices are 32-bit elements; how exact they have to be, the bound alone decides.
No kernel may reach another device: no remote copies, remote signals or barrier semaphores. Data moves between devices by JAX's collectives and lax.ppermute only.
A program may use at most 128 MiB of HBM per device.

```python
import math
import jax
import jax.numpy as jnp
import numpy as np
from jax import lax

PAD = 4096
CELL = 8
NCOL = 2
GRID = 2048
CELLS = 256
SURF = 64
Q = 384
MOST = 4
SLOTS = 512
N_ROW = 128


def reversed_index(values, axis):
    return jnp.roll(jnp.flip(values, axis), 1, axis)


def draw_green_spectrum(key, part):
    uniform_base = jax.random.uniform(key, (PAD, PAD), jnp.float32)
    symmetric = 0.25 + 0.5 * (uniform_base + uniform_base.T)
    even_rows = 0.5 * (symmetric + reversed_index(symmetric, 0))
    return 0.5 * (even_rows + reversed_index(even_rows, 1))


def plant(values, stream_key, low, largest):
    shape = values.shape
    place = [jax.random.randint(jax.random.fold_in(stream_key, axis), (), 0, shape[axis]) for axis in range(len(shape))]
    values = values.at[tuple(place)].set(low)
    longest = shape.index(max(shape))
    place[longest] = (place[longest] + 1) % shape[longest]
    return values.at[tuple(place)].set(largest)


def level_of(own_key, extent, shards, low, largest):
    def one(dim, shards_of):
        draws = jax.random.uniform(jax.random.fold_in(jax.random.fold_in(own_key, 6), dim), (shards_of,), jnp.float32, low / len(shards), largest / len(shards))
        return jnp.repeat(jnp.exp(draws), extent[dim] // shards_of).reshape((-1,) + (1,) * (len(extent) - dim - 1))

    gain = one(*shards[0])
    for cut in shards[1:]:
        gain = gain * one(*cut)
    return gain


def split_up(number_of, total, reach, lean):
    portions = [(1 << 20) // math.isqrt(grade ** lean) + 1 for grade in range(2, number_of + 1)]
    surplus, holding = total - reach - (number_of - 1), [1] * (number_of - 1)
    while surplus > 0:
        movable = [i for i in range(number_of - 1) if holding[i] < reach]
        whole, left = sum([portions[i] for i in movable]), surplus
        for i in movable:
            extra = min(reach - holding[i], max(1, left * portions[i] // whole), surplus)
            holding[i] = holding[i] + extra
            surplus = surplus - extra
    return np.array([reach] + holding)


def uneven(key, count, total, most, lean):
    if count == 2:
        one = jax.random.randint(key, (), max(1, total - most), min(most, total - 1) + 1)
        return jnp.stack([one, total - one])
    sizes = jnp.asarray(split_up(count, total, most, lean), jnp.int32)
    pairs = (count - 1) // 2
    source_of, receiver = sizes[1:1 + 2 * pairs:2], sizes[2:2 + 2 * pairs:2]
    slack = jnp.minimum(source_of - 1, most - receiver)
    moved = jax.random.randint(jax.random.fold_in(key, 1), (pairs,), 0, 1 << 20) % (slack + 1)
    sizes = sizes.at[1:1 + 2 * pairs:2].set(source_of - moved).at[2:2 + 2 * pairs:2].set(receiver + moved)
    return sizes[jax.random.permutation(jax.random.fold_in(key, 2), count)]


def centred(rng, extent, deviation, most, cuts=(), held_as=jnp.bfloat16):
    drawn = deviation * jax.random.normal(rng, extent, jnp.float32)
    if cuts:
        drawn = drawn * level_of(rng, extent, cuts, -0.22, 0.18)
    return jnp.clip(drawn, -most, most).astype(held_as)


def setup_inputs(seed: int = 0) -> dict:
    key_list = jax.random.split(jax.random.key(seed), 8)
    return {
        "displacement": centred(key_list[0], (SLOTS, CELLS, NCOL, Q), 1.0, 6.0, ((0, 128),), jnp.float32),
        "stiffness": centred(key_list[1], (Q, Q), Q ** -0.5, 0.3125),
        "coupling": jnp.clip(jax.random.uniform(key_list[2], (Q,), jnp.float32, 0.1, 0.5), 0.1, 0.5),
        "softening": jnp.clip(jnp.exp(jax.random.uniform(key_list[3], (Q,), jnp.float32, math.log(0.2), math.log(2.0))), 0.2, 2.0),
        "electrode_mask": plant((jax.random.randint(key_list[4], (SLOTS, CELLS), 0, 2) < 1).astype(jnp.int32), jax.random.fold_in(key_list[4], 1), 0, 1),
        "row_counts": uneven(key_list[5], N_ROW, CELLS, MOST, 2).astype(jnp.int32),
        "green_spectrum": draw_green_spectrum(jax.random.fold_in(key_list[7], 71), 0),
    }


def reference(displacement, stiffness, coupling, softening, electrode_mask, row_counts, green_spectrum):
    starts = (jnp.cumsum(row_counts) - row_counts).astype(jnp.int32)
    cell_rows = jnp.arange(CELLS, dtype=jnp.int32)
    owners = jnp.sum((starts[None, :] <= cell_rows[:, None]).astype(jnp.int32), axis=1) - 1
    slot_index = (owners * MOST + cell_rows - starts[owners]).astype(jnp.int32)
    by_cell = displacement[slot_index]
    electrode = electrode_mask[slot_index].astype(jnp.float32)
    rounded = by_cell.astype(jnp.bfloat16)
    elastic = jnp.dot(rounded.reshape(-1, Q).astype(jnp.float32), stiffness.astype(jnp.float32),
                      precision=lax.Precision.HIGHEST).reshape(by_cell.shape)
    framed = jnp.pad(by_cell, ((1, 1), (1, 1), (0, 0), (0, 0)))
    beside = framed[:-2, 1:-1] + framed[2:, 1:-1] + framed[1:-1, :-2] + framed[1:-1, 2:]
    structural = elastic - coupling * beside - electrode[:, :, None, None] * softening * by_cell
    surface = by_cell[..., :SURF].reshape(CELLS, CELLS, NCOL, CELL, CELL)
    surface = surface.transpose(2, 0, 3, 1, 4).reshape(NCOL, GRID, GRID)

    def convolve(surface_plane):
        spread = jnp.pad(surface_plane, ((0, PAD - GRID), (0, PAD - GRID)))
        spectrum = jnp.fft.fft2(spread) * green_spectrum
        return jnp.real(jnp.fft.ifft2(spectrum))[:GRID, :GRID]

    pressure = lax.map(convolve, surface)
    pressure_dofs = pressure.reshape(NCOL, CELLS, CELL, CELLS, CELL).transpose(1, 3, 0, 2, 4)
    pressure_dofs = pressure_dofs.reshape(CELLS, CELLS, NCOL, SURF)
    load_cells = jnp.concatenate([structural[..., :SURF] + pressure_dofs, structural[..., SURF:]], axis=-1)
    return jnp.zeros_like(displacement).at[slot_index].set(load_cells)
```

```python
import math

import jax
import jax.numpy as jnp
import numpy as np
from jax import lax
from jax.experimental import pallas as pl
from jax.experimental.pallas import tpu as pltpu
from jax.sharding import PartitionSpec as P

CELL = 8
HALF = 512
CELLS = 256
PAD = 4096
SLOTS = 4
DEVICES = 128
VMEM_LIMIT = 48 * 1024 * 1024
F32 = jnp.float32
BF16 = jnp.bfloat16


def hi_lo_constant(values):
    values = np.asarray(values, np.float32)
    high = values.astype(jnp.bfloat16)
    low = (values - high.astype(np.float32)).astype(jnp.bfloat16)
    return np.stack([high, low])


def dft_table():
    cell = np.arange(CELLS)[:, None]
    freq = np.arange(HALF)[None, :]
    phase = (cell * freq % HALF) * (2.0 * math.pi / HALF)
    return hi_lo_constant(np.concatenate([np.cos(phase), np.sin(phase)], axis=0))


def twiddle_table():
    point = np.arange(CELL)[:, None]
    freq = np.arange(HALF)[None, :]
    phase = point * freq * (2.0 * math.pi / PAD)
    return np.concatenate([np.cos(phase), np.sin(phase)], axis=0).astype(np.float32)


def dof_order_table(scale):
    table = np.zeros((CELL, CELL, SLOTS, SLOTS, 128), np.float32)
    for b in range(CELL):
        for a in range(CELL):
            for slot in range(SLOTS):
                table[b, a, slot, slot, a * CELL + b] = scale
    return table.reshape(CELL * CELL * SLOTS, SLOTS * 128).astype(jnp.bfloat16)


def split(values):
    high = values.astype(BF16)
    return high, (values - high.astype(F32)).astype(BF16)


def dot(left, right):
    return jnp.dot(left, right, preferred_element_type=F32)


def dot_nt(left, right):
    return lax.dot_general(left, right, (((1,), (1,)), ((), ())), preferred_element_type=F32)


def dot3(left, right_ref):
    high, low = split(left)
    return dot(high, right_ref[0]) + (dot(high, right_ref[1]) + dot(low, right_ref[0]))


def dot3_nt(left_high, left_low, right):
    high, low = split(right)
    return dot_nt(left_high, high) + (dot_nt(left_high, low) + dot_nt(left_low, high))


ROOT = math.sqrt(0.5)


def cadd(x, y):
    return (x[0] + y[0], x[1] + y[1])


def csub(x, y):
    return (x[0] - y[0], x[1] - y[1])


def turn(x, eighths, sign):
    re, im = x
    if eighths == 0:
        return x
    if eighths == 2:
        return (-im, re) if sign > 0 else (im, -re)
    if eighths == 1:
        return ((re - im) * ROOT, (im + re) * ROOT) if sign > 0 else ((re + im) * ROOT, (im - re) * ROOT)
    return ((-re - im) * ROOT, (re - im) * ROOT) if sign > 0 else ((im - re) * ROOT, (-re - im) * ROOT)


def dft4(x, sign):
    s0, d0 = cadd(x[0], x[2]), csub(x[0], x[2])
    s1, d1 = cadd(x[1], x[3]), turn(csub(x[1], x[3]), 2, sign)
    return [cadd(s0, s1), cadd(d0, d1), csub(s0, s1), csub(d0, d1)]


def dft8(x, sign):
    even = dft4([cadd(x[n], x[n + 4]) for n in range(4)], sign)
    odd = dft4([turn(csub(x[n], x[n + 4]), n, sign) for n in range(4)], sign)
    return [v for pair in zip(even, odd) for v in pair]


def twist(x, cos, sin, sign):
    re, im = x
    if sign > 0:
        return (re * cos - im * sin, im * cos + re * sin)
    return (re * cos + im * sin, im * cos - re * sin)


def swap_groups(tiles, lane):
    low_half = lane < 64
    t0, t1, t2, t3 = tiles
    u0 = jnp.where(low_half, t0, pltpu.roll(t2, 64, 1))
    u2 = jnp.where(low_half, pltpu.roll(t0, 64, 1), t2)
    u1 = jnp.where(low_half, t1, pltpu.roll(t3, 64, 1))
    u3 = jnp.where(low_half, pltpu.roll(t1, 64, 1), t3)
    even = lax.rem(lane, 64) < 32
    return [
        jnp.where(even, u0, pltpu.roll(u1, 32, 1)),
        jnp.where(even, pltpu.roll(u0, 96, 1), u1),
        jnp.where(even, u2, pltpu.roll(u3, 32, 1)),
        jnp.where(even, pltpu.roll(u2, 96, 1), u3),
    ]


def tile(ref, part, block, row, lane_tile):
    start = part * 256 + block * 32 + row * 8
    return ref.at[start:start + 8, lane_tile * 128:lane_tile * 128 + 128]


def forward_kernel(x_ref, order_ref, table_ref, twist_ref, out_ref, y_ref):
    planes = []
    for c in range(2):
        plane = jnp.concatenate([x_ref[slot, :, c, :] for slot in range(SLOTS)], axis=1)
        high, low = split(plane)
        planes.append(dot_nt(order_ref[...], high) + dot_nt(order_ref[...], low))
    w0, w1 = planes
    stacked = jnp.concatenate(
        [jnp.concatenate([w0, w1], axis=1), jnp.concatenate([w1, -w0], axis=1)], axis=0
    )
    y_ref[...] = dot3(stacked, table_ref)
    lane = lax.broadcasted_iota(jnp.int32, (8, 128), 1)
    for lane_tile in range(4):
        cut = slice(lane_tile * 128, lane_tile * 128 + 128)
        for row in range(4):
            points = []
            for b in range(CELL):
                value = tuple(tile(y_ref, o, b, row, lane_tile)[...] for o in range(2))
                if b:
                    value = twist(value, twist_ref[b:b + 1, cut], twist_ref[8 + b:9 + b, cut], -1)
                points.append(value)
            for k, value in enumerate(dft8(points, -1)):
                for o in range(2):
                    tile(y_ref, o, k, row, lane_tile)[...] = value[o]
        for k in range(CELL):
            for o in range(2):
                tiles = [tile(y_ref, o, k, row, lane_tile)[...] for row in range(4)]
                for u, value in enumerate(swap_groups(tiles, lane)):
                    out_ref[k * 16 + lane_tile * 4 + u, o * 8:o * 8 + 8, :] = value


def middle_kernel(x_ref, across_ref, down_ref, table_ref, twist_ref, green_ref, out_ref, y_ref):
    rows = jnp.concatenate(
        [x_ref[:, c * 8:c * 8 + 8, :].reshape(1024, 128) for c in range(2)], axis=1
    )
    high, low = split(rows)
    place = lax.broadcasted_iota(jnp.int32, (512, 1024), 0)
    chosen = jnp.where(place == across_ref[...], 1.0, 0.0).astype(BF16)
    compact = dot(chosen, high) + dot(chosen, low)
    w = [
        jnp.concatenate(
            [compact[h * 256:h * 256 + 256, c * 128:c * 128 + 128].T for h in range(2)], axis=0
        )
        for c in range(2)
    ]
    stacked = jnp.concatenate(
        [jnp.concatenate([w[0], w[1]], axis=1), jnp.concatenate([w[1], -w[0]], axis=1)], axis=0
    )
    y_ref[...] = dot3(stacked, table_ref)
    for lane_tile in range(4):
        cut = slice(lane_tile * 128, lane_tile * 128 + 128)
        for row in range(4):
            points = []
            for a in range(CELL):
                block = (a % 2) * 4 + a // 2
                value = tuple(tile(y_ref, o, block, row, lane_tile)[...] for o in range(2))
                if a:
                    value = twist(value, twist_ref[a:a + 1, cut], twist_ref[8 + a:9 + a, cut], -1)
                points.append(value)
            spectrum = []
            for q, value in enumerate(dft8(points, -1)):
                first = q * 512 + lane_tile * 128
                green = green_ref[row * 8:row * 8 + 8, first:first + 128]
                spectrum.append((value[0] * green, value[1] * green))
            for a, value in enumerate(dft8(spectrum, 1)):
                block = (a % 2) * 4 + a // 2
                if a:
                    value = twist(value, twist_ref[a:a + 1, cut], twist_ref[8 + a:9 + a, cut], 1)
                for o in range(2):
                    tile(y_ref, o, block, row, lane_tile)[...] = value[o]
    back = inverse_cells(y_ref, table_ref)
    pieces = [
        jnp.concatenate(
            [back[:, c * 256 + h * 128:c * 256 + h * 128 + 128] for c in range(2)], axis=1
        )
        for h in range(2)
    ]
    high, low = split(jnp.concatenate(pieces, axis=0))
    place = lax.broadcasted_iota(jnp.int32, (1024, 128), 1)
    down = down_ref[...]
    spread = jnp.concatenate(
        [jnp.where(place + 128 * n == down, 1.0, 0.0).astype(BF16) for n in range(4)], axis=1
    )
    result = dot(spread, high) + dot(spread, low)
    for c in range(2):
        out_ref[:, c * 8:c * 8 + 8, :] = result[:, c * 128:c * 128 + 128].reshape(128, 8, 128)


def inverse_cells(y_ref, table_ref):
    re, im = y_ref[0:256, :], y_ref[256:512, :]
    by_cos = jnp.concatenate([re, im], axis=0)
    by_sin = jnp.concatenate([-im, re], axis=0)
    return dot3_nt(table_ref[0, 0:256, :], table_ref[1, 0:256, :], by_cos) + dot3_nt(
        table_ref[0, 256:512, :], table_ref[1, 256:512, :], by_sin
    )


def backward_kernel(x_ref, part_ref, order_ref, table_ref, twist_ref, out_ref, y_ref):
    lane = lax.broadcasted_iota(jnp.int32, (8, 128), 1)
    for lane_tile in range(4):
        cut = slice(lane_tile * 128, lane_tile * 128 + 128)
        for k in range(CELL):
            for o in range(2):
                tiles = [x_ref[k * 16 + lane_tile * 4 + u, o * 8:o * 8 + 8, :] for u in range(4)]
                for row, value in enumerate(swap_groups(tiles, lane)):
                    tile(y_ref, o, k, row, lane_tile)[...] = value
        for row in range(4):
            points = [
                tuple(tile(y_ref, o, k, row, lane_tile)[...] for o in range(2))
                for k in range(CELL)
            ]
            for b, value in enumerate(dft8(points, 1)):
                if b:
                    value = twist(value, twist_ref[b:b + 1, cut], twist_ref[8 + b:9 + b, cut], 1)
                for o in range(2):
                    tile(y_ref, o, b, row, lane_tile)[...] = value[o]
    back = inverse_cells(y_ref, table_ref)
    for c in range(2):
        high, low = split(back[:, c * 256:c * 256 + 256])
        plane = dot(high, order_ref[...]) + dot(low, order_ref[...])
        for slot in range(SLOTS):
            out_ref[slot, :, c, :] = (
                part_ref[slot, :, c, :] + plane[:, slot * 128:slot * 128 + 128]
            )


def structural_kernel(
    count_ref, x_ref, above_ref, below_ref, stiff_ref, couple_ref, soft_ref, mask_ref, out_ref
):
    count = count_ref[0]
    cell = lax.broadcasted_iota(jnp.int32, (CELLS, 1), 0)
    for slot in range(SLOTS):
        biased = mask_ref[:, slot:slot + 1]
        used = slot < count
        last = slot == count - 1
        for c in range(2):
            own = x_ref[slot, :, c, :]
            elastic = dot(own.astype(BF16), stiff_ref[...])
            before = above_ref[:, c, :] if slot == 0 else x_ref[slot - 1, :, c, :]
            after = below_ref[:, c, :]
            if slot < SLOTS - 1:
                after = jnp.where(last, after, x_ref[slot + 1, :, c, :])
            left = jnp.where(cell == 0, 0.0, pltpu.roll(own, 1, 0))
            right = jnp.where(cell == CELLS - 1, 0.0, pltpu.roll(own, CELLS - 1, 0))
            beside = before + after + left + right
            value = elastic - couple_ref[...] * beside - (biased * soft_ref[...]) * own
            out_ref[slot, :, c, :] = jnp.where(used, value, 0.0)


def whole(*shape):
    return pl.BlockSpec(shape, lambda i: (0,) * len(shape))


def per_device(
    displacement, stiffness, coupling, softening, electrode_mask, row_counts, green_spectrum
):
    devices = lax.axis_size("row")
    position = lax.axis_index("row")
    table = jnp.asarray(dft_table())
    turns = jnp.asarray(twiddle_table())
    params = pltpu.CompilerParams(vmem_limit_bytes=VMEM_LIMIT)
    surface_block = pl.BlockSpec((SLOTS, CELLS, 2, 128), lambda i: (0, 0, 0, 0))
    own_count = row_counts[position]
    up = [(i, i + 1) for i in range(devices - 1)]
    down = [(j, i) for i, j in up]
    last_used = lax.dynamic_slice_in_dim(displacement, own_count - 1, 1, 0)
    above = lax.ppermute(last_used, "row", up)
    below = lax.ppermute(displacement[:1], "row", down)

    sent = pl.pallas_call(
        forward_kernel,
        grid=(1,),
        in_specs=[surface_block, whole(256, 512), whole(2, 512, 512), whole(16, 512)],
        out_specs=whole(DEVICES, 16, 128),
        out_shape=jax.ShapeDtypeStruct((DEVICES, 16, 128), F32),
        scratch_shapes=[pltpu.VMEM((512, 512), F32)],
        compiler_params=params,
        cost_estimate=pl.CostEstimate(flops=10**9, bytes_accessed=4 << 20, transcendentals=0),
    )(displacement, jnp.asarray(dof_order_table(1.0)), table, turns)
    received = lax.all_to_all(sent, "row", split_axis=0, concat_axis=0, tiled=True)

    before = jnp.arange(DEVICES)[:, None] > jnp.arange(DEVICES)[None, :]
    starts = jnp.sum(jnp.where(before, row_counts[None, :], 0), axis=1)
    half = jnp.arange(2, dtype=jnp.int32)[None, :, None]
    slot = jnp.arange(SLOTS, dtype=jnp.int32)[None, None, :]
    cell_row = starts[:, None, None] + slot
    place = jnp.where(slot < row_counts[:, None, None], half * CELLS + cell_row, -1)
    place = place.reshape(1024).astype(jnp.int32)
    across = place.reshape(1, 1024)
    downward = jnp.broadcast_to(place[:, None], (1024, 128))

    sent = pl.pallas_call(
        middle_kernel,
        grid=(1,),
        in_specs=[
            whole(DEVICES, 16, 128), whole(1, 1024), whole(1024, 128),
            whole(2, 512, 512), whole(16, 512), whole(32, PAD),
        ],
        out_specs=whole(DEVICES, 16, 128),
        out_shape=jax.ShapeDtypeStruct((DEVICES, 16, 128), F32),
        scratch_shapes=[pltpu.VMEM((512, 512), F32)],
        compiler_params=params,
        cost_estimate=pl.CostEstimate(flops=3 * 10**9, bytes_accessed=5 << 20, transcendentals=0),
    )(received, across, downward, table, turns, green_spectrum)
    received = lax.all_to_all(sent, "row", split_axis=0, concat_axis=0, tiled=True)

    full_block = whole(SLOTS, CELLS, 2, 384)
    structural = pl.pallas_call(
        structural_kernel,
        grid=(1,),
        in_specs=[
            pl.BlockSpec(memory_space=pltpu.SMEM),
            full_block, whole(CELLS, 2, 384), whole(CELLS, 2, 384), whole(384, 384),
            whole(1, 384), whole(1, 384), whole(CELLS, SLOTS),
        ],
        out_specs=full_block,
        out_shape=jax.ShapeDtypeStruct(displacement.shape, F32),
        compiler_params=params,
        cost_estimate=pl.CostEstimate(flops=10**9, bytes_accessed=8 << 20, transcendentals=0),
    )(
        own_count.reshape(1), displacement, above[0], below[0], stiffness,
        coupling[None, :], softening[None, :], electrode_mask.astype(F32).T,
    )
    return pl.pallas_call(
        backward_kernel,
        grid=(1,),
        in_specs=[
            whole(DEVICES, 16, 128), surface_block, whole(256, 512),
            whole(2, 512, 512), whole(16, 512),
        ],
        out_specs=surface_block,
        out_shape=jax.ShapeDtypeStruct(displacement.shape, F32),
        scratch_shapes=[pltpu.VMEM((512, 512), F32)],
        input_output_aliases={1: 0},
        compiler_params=params,
        cost_estimate=pl.CostEstimate(flops=10**9, bytes_accessed=4 << 20, transcendentals=0),
    )(received, structural, jnp.asarray(dof_order_table(1.0 / (PAD * PAD))), table, turns)


def solution(mesh):
    placed = (P("row", None, None, None), P(), P(), P(), P("row", None), P(), P("row", None))
    return jax.shard_map(
        per_device,
        mesh=mesh,
        in_specs=placed,
        out_specs=P("row", None, None, None),
        check_vma=False,
    )
```

```python
import math

import jax
import jax.numpy as jnp
import numpy as np
from jax import lax
from jax.experimental import pallas as pl
from jax.experimental.pallas import tpu as pltpu
from jax.sharding import PartitionSpec as P

CELL = 8
HALF = 512
CELLS = 256
PAD = 4096
SLOTS = 4
DEVICES = 128
VMEM_LIMIT = 60 * 1024 * 1024
F32 = jnp.float32
BF16 = jnp.bfloat16


def hi_lo_constant(values):
    values = np.asarray(values, np.float32)
    high = values.astype(jnp.bfloat16)
    low = (values - high.astype(np.float32)).astype(jnp.bfloat16)
    return np.stack([high, low])


def dft_table():
    cell = np.arange(CELLS)[:, None]
    freq = np.arange(HALF)[None, :]
    phase = (cell * freq % HALF) * (2.0 * math.pi / HALF)
    return hi_lo_constant(np.concatenate([np.cos(phase), np.sin(phase)], axis=0))


def twiddle_table():
    point = np.arange(CELL)[:, None]
    freq = np.arange(HALF)[None, :]
    phase = point * freq * (2.0 * math.pi / PAD)
    return np.concatenate([np.cos(phase), np.sin(phase)], axis=0).astype(np.float32)


def dof_order_table(scale):
    table = np.zeros((CELL, CELL // 2, SLOTS, 2, SLOTS, 128), np.float32)
    for b in range(CELL):
        for a in range(CELL):
            for slot in range(SLOTS):
                table[b, a // 2, slot, a % 2, slot, a * CELL + b] = scale
    return table.reshape(CELL * CELL * SLOTS, SLOTS * 128).astype(jnp.bfloat16)


def split(values):
    high = values.astype(BF16)
    return high, (values - high.astype(F32)).astype(BF16)


def dot(left, right):
    return jnp.dot(left, right, preferred_element_type=F32)


def dot_nt(left, right):
    return lax.dot_general(left, right, (((1,), (1,)), ((), ())), preferred_element_type=F32)


def dot3(left, right_ref):
    high, low = split(left)
    return dot(high, right_ref[0]) + (dot(high, right_ref[1]) + dot(low, right_ref[0]))


def dot3_nt(left_high, left_low, right):
    high, low = split(right)
    return dot_nt(left_high, high) + (dot_nt(left_high, low) + dot_nt(left_low, high))


ROOT = math.sqrt(0.5)


def cadd(x, y):
    return (x[0] + y[0], x[1] + y[1])


def csub(x, y):
    return (x[0] - y[0], x[1] - y[1])


def turn(x, eighths, sign):
    re, im = x
    if eighths == 0:
        return x
    if eighths == 2:
        return (-im, re) if sign > 0 else (im, -re)
    if eighths == 1:
        return ((re - im) * ROOT, (im + re) * ROOT) if sign > 0 else ((re + im) * ROOT, (im - re) * ROOT)
    return ((-re - im) * ROOT, (re - im) * ROOT) if sign > 0 else ((im - re) * ROOT, (-re - im) * ROOT)


def dft4(x, sign):
    s0, d0 = cadd(x[0], x[2]), csub(x[0], x[2])
    s1, d1 = cadd(x[1], x[3]), turn(csub(x[1], x[3]), 2, sign)
    return [cadd(s0, s1), cadd(d0, d1), csub(s0, s1), csub(d0, d1)]


def dft8(x, sign):
    even = dft4([cadd(x[n], x[n + 4]) for n in range(4)], sign)
    odd = dft4([turn(csub(x[n], x[n + 4]), n, sign) for n in range(4)], sign)
    return [v for pair in zip(even, odd) for v in pair]


def twist(x, cos, sin, sign):
    re, im = x
    if sign > 0:
        return (re * cos - im * sin, im * cos + re * sin)
    return (re * cos + im * sin, im * cos - re * sin)


def swap_groups(tiles, lane):
    low_half = lane < 64
    t0, t1, t2, t3 = tiles
    u0 = jnp.where(low_half, t0, pltpu.roll(t2, 64, 1))
    u2 = jnp.where(low_half, pltpu.roll(t0, 64, 1), t2)
    u1 = jnp.where(low_half, t1, pltpu.roll(t3, 64, 1))
    u3 = jnp.where(low_half, pltpu.roll(t1, 64, 1), t3)
    even = lax.rem(lane, 64) < 32
    return [
        jnp.where(even, u0, pltpu.roll(u1, 32, 1)),
        jnp.where(even, pltpu.roll(u0, 96, 1), u1),
        jnp.where(even, u2, pltpu.roll(u3, 32, 1)),
        jnp.where(even, pltpu.roll(u2, 96, 1), u3),
    ]


def tile(ref, part, block, row, lane_tile):
    start = part * 256 + block * 32 + row * 8
    return ref.at[start:start + 8, lane_tile * 128:lane_tile * 128 + 128]


def fetch(sources, targets, sems):
    copies = [
        pltpu.make_async_copy(source, target, sems.at[n])
        for n, (source, target) in enumerate(zip(sources, targets))
    ]
    for copy in copies:
        copy.start()
    return copies


def forward_kernel(
    x_hbm, order_hbm, table_hbm, twist_hbm, out_hbm,
    x_ref, order_ref, table_ref, twist_ref, out_ref, y_ref, sems, out_sems,
):
    copies = fetch(
        [x_hbm.at[slot] for slot in range(SLOTS)] + [order_hbm, table_hbm, twist_hbm],
        [x_ref.at[slot] for slot in range(SLOTS)] + [order_ref, table_ref, twist_ref],
        sems,
    )
    for copy in copies[:5]:
        copy.wait()
    planes = []
    for c in range(2):
        plane = jnp.concatenate([x_ref[slot, :, c, 0:128] for slot in range(SLOTS)], axis=1)
        high, low = split(plane)
        planes.append(dot_nt(order_ref[...], high) + dot_nt(order_ref[...], low))
    w0, w1 = planes
    stacked = jnp.concatenate(
        [jnp.concatenate([w0, w1], axis=1), jnp.concatenate([w1, -w0], axis=1)], axis=0
    )
    copies[5].wait()
    y_ref[...] = dot3(stacked, table_ref)
    copies[6].wait()
    lane = lax.broadcasted_iota(jnp.int32, (64, 128), 1)
    outs = []
    for lane_tile in range(4):
        cut = slice(lane_tile * 128, lane_tile * 128 + 128)
        for row in range(4):
            points = []
            for b in range(CELL):
                value = tuple(tile(y_ref, o, b, row, lane_tile)[...] for o in range(2))
                if b:
                    value = twist(value, twist_ref[b:b + 1, cut], twist_ref[8 + b:9 + b, cut], -1)
                points.append(value)
            for k, value in enumerate(dft8(points, -1)):
                for o in range(2):
                    tile(y_ref, o, k, row, lane_tile)[...] = value[o]
        for o in range(2):
            block = y_ref[o * 256:o * 256 + 256, cut].reshape(8, 4, 8, 128)
            tiles = [block[:, row].reshape(64, 128) for row in range(4)]
            for u, value in enumerate(swap_groups(tiles, lane)):
                out_ref[:, lane_tile * 4 + u, o * 8:o * 8 + 8, :] = value.reshape(8, 8, 128)
        here = slice(lane_tile * 4, lane_tile * 4 + 4)
        copy = pltpu.make_async_copy(
            out_ref.at[:, here], out_hbm.at[:, here], out_sems.at[lane_tile]
        )
        copy.start()
        outs.append(copy)
    for copy in outs:
        copy.wait()


def middle_kernel(
    counts_ref, x_hbm, table_hbm, twist_hbm, green_hbm, out_hbm,
    x_ref, table_ref, twist_ref, green_ref, out_ref, cells_ref, y_ref, sems, out_sems,
):
    copies = fetch(
        (x_hbm, table_hbm, twist_hbm, green_hbm), (x_ref, table_ref, twist_ref, green_ref), sems
    )
    copies[0].wait()

    def gather(device, start):
        for c in range(2):
            cells_ref[c, pl.ds(start, SLOTS)] = x_ref[device, c]
        return start + counts_ref[device]

    lax.fori_loop(0, DEVICES, gather, 0, unroll=8)
    w = [
        jnp.concatenate([cells_ref[c, 0:CELLS, h, :].T for h in range(2)], axis=0)
        for c in range(2)
    ]
    stacked = jnp.concatenate(
        [jnp.concatenate([w[0], w[1]], axis=1), jnp.concatenate([w[1], -w[0]], axis=1)], axis=0
    )
    copies[1].wait()
    y_ref[...] = dot3(stacked, table_ref)
    copies[2].wait()
    copies[3].wait()
    for lane_tile in range(4):
        cut = slice(lane_tile * 128, lane_tile * 128 + 128)
        for row in range(4):
            points = []
            for a in range(CELL):
                block = (a % 2) * 4 + a // 2
                value = tuple(tile(y_ref, o, block, row, lane_tile)[...] for o in range(2))
                if a:
                    value = twist(value, twist_ref[a:a + 1, cut], twist_ref[8 + a:9 + a, cut], -1)
                points.append(value)
            spectrum = []
            for q, value in enumerate(dft8(points, -1)):
                first = q * 512 + lane_tile * 128
                green = green_ref[row * 8:row * 8 + 8, first:first + 128]
                spectrum.append((value[0] * green, value[1] * green))
            for a, value in enumerate(dft8(spectrum, 1)):
                block = (a % 2) * 4 + a // 2
                if a:
                    value = twist(value, twist_ref[a:a + 1, cut], twist_ref[8 + a:9 + a, cut], 1)
                for o in range(2):
                    tile(y_ref, o, block, row, lane_tile)[...] = value[o]
    back = inverse_cells(y_ref, table_ref)
    for c in range(2):
        cells_ref[c, CELLS:] = jnp.zeros((8, 2, 128), F32)
        for h in range(2):
            first = (c * 2 + h) * 128
            cells_ref[c, 0:CELLS, h, :] = back[:, first:first + 128]

    slot = lax.broadcasted_iota(jnp.int32, (SLOTS, 2, 128), 0)

    def scatter(device, start):
        count = counts_ref[device]
        for c in range(2):
            held = cells_ref[c, pl.ds(start, SLOTS)]
            out_ref[device, c] = jnp.where(slot < count, held, 0.0)
        return start + count

    outs = []
    start = 0
    for part in range(4):
        here = slice(part * 32, part * 32 + 32)
        start = lax.fori_loop(part * 32, part * 32 + 32, scatter, start, unroll=8)
        copy = pltpu.make_async_copy(out_ref.at[here], out_hbm.at[here], out_sems.at[part])
        copy.start()
        outs.append(copy)
    for copy in outs:
        copy.wait()


def inverse_cells(y_ref, table_ref):
    re, im = y_ref[0:256, :], y_ref[256:512, :]
    by_cos = jnp.concatenate([re, im], axis=0)
    by_sin = jnp.concatenate([-im, re], axis=0)
    return dot3_nt(table_ref[0, 0:256, :], table_ref[1, 0:256, :], by_cos) + dot3_nt(
        table_ref[0, 256:512, :], table_ref[1, 256:512, :], by_sin
    )


def backward_kernel(
    x_hbm, whole_hbm, part_hbm, order_hbm, table_hbm, twist_hbm, out_hbm,
    x_ref, part_ref, order_ref, table_ref, twist_ref, out_ref, y_ref, sems, out_sems,
):
    copies = fetch(
        (x_hbm, twist_hbm, table_hbm, order_hbm, part_hbm),
        (x_ref, twist_ref, table_ref, order_ref, part_ref),
        sems,
    )
    lane = lax.broadcasted_iota(jnp.int32, (64, 128), 1)
    copies[0].wait()
    copies[1].wait()
    for lane_tile in range(4):
        cut = slice(lane_tile * 128, lane_tile * 128 + 128)
        for o in range(2):
            tiles = [
                x_ref[:, lane_tile * 4 + u, o * 8:o * 8 + 8, :].reshape(64, 128) for u in range(4)
            ]
            for row, value in enumerate(swap_groups(tiles, lane)):
                for k in range(CELL):
                    tile(y_ref, o, k, row, lane_tile)[...] = value[k * 8:k * 8 + 8, :]
        for row in range(4):
            points = [
                tuple(tile(y_ref, o, k, row, lane_tile)[...] for o in range(2))
                for k in range(CELL)
            ]
            for b, value in enumerate(dft8(points, 1)):
                if b:
                    value = twist(value, twist_ref[b:b + 1, cut], twist_ref[8 + b:9 + b, cut], 1)
                for o in range(2):
                    tile(y_ref, o, b, row, lane_tile)[...] = value[o]
    copies[2].wait()
    back = inverse_cells(y_ref, table_ref)
    copies[3].wait()
    copies[4].wait()
    halves = [split(back[:, c * 256:c * 256 + 256]) for c in range(2)]
    outs = []
    for slot in range(SLOTS):
        order = order_ref[:, slot * 128:slot * 128 + 128]
        for c in range(2):
            plane = dot(halves[c][0], order) + dot(halves[c][1], order)
            out_ref[slot, :, c, :] = part_ref[slot, c] + plane
        copy = pltpu.make_async_copy(
            out_ref.at[slot], out_hbm.at[slot, :, :, 0:128], out_sems.at[slot]
        )
        copy.start()
        outs.append(copy)
    for copy in outs:
        copy.wait()


def edge_kernel(counts_ref, x_hbm, first_hbm, last_hbm, first_ref, last_ref, sems, out_sems):
    count = counts_ref[lax.axis_index("row")]
    ins = fetch((x_hbm.at[0:1], x_hbm.at[pl.ds(count - 1, 1)]), (first_ref, last_ref), sems)
    outs = []
    for n, (held, target) in enumerate(((first_ref, first_hbm), (last_ref, last_hbm))):
        ins[n].wait()
        copy = pltpu.make_async_copy(held, target, out_sems.at[n])
        copy.start()
        outs.append(copy)
    for copy in outs:
        copy.wait()


def structural_kernel(
    counts_ref, x_hbm, above_hbm, below_hbm, stiff_hbm, couple_ref, soft_ref, mask_ref,
    out_hbm, part_hbm, x_ref, above_ref, below_ref, stiff_ref, plane_ref, part_ref, sems, out_sems,
):
    count = counts_ref[lax.axis_index("row")]
    copies = fetch(
        [stiff_hbm, above_hbm, below_hbm] + [x_hbm.at[slot] for slot in range(SLOTS)],
        [stiff_ref, above_ref, below_ref] + [x_ref.at[slot] for slot in range(SLOTS)],
        sems,
    )
    for slot in range(SLOTS):
        copies[3 + slot].wait()
        for c in range(2):
            plane_ref[slot + 1, c] = x_ref[slot, :, c, :]
    for copy in copies[:3]:
        copy.wait()
    for c in range(2):
        plane_ref[0, c] = above_ref[0, :, c, :]
        plane_ref[count + 1, c] = below_ref[0, :, c, :]
    outs = []
    cell = lax.broadcasted_iota(jnp.int32, (CELLS, 1), 0)
    for slot in range(SLOTS):
        biased = mask_ref[:, slot:slot + 1]
        for c in range(2):
            own = plane_ref[slot + 1, c]
            elastic = dot(own.astype(BF16), stiff_ref[...])
            left = jnp.where(cell == 0, 0.0, pltpu.roll(own, 1, 0))
            right = jnp.where(cell == CELLS - 1, 0.0, pltpu.roll(own, CELLS - 1, 0))
            beside = plane_ref[slot, c] + plane_ref[slot + 2, c] + left + right
            value = elastic - couple_ref[...] * beside - (biased * soft_ref[...]) * own
            value = jnp.where(slot < count, value, 0.0)
            part_ref[slot, c] = value[:, 0:128]
            x_ref[slot, :, c, :] = value
        copy = pltpu.make_async_copy(x_ref.at[slot], out_hbm.at[slot], out_sems.at[slot])
        copy.start()
        outs.append(copy)
    copy = pltpu.make_async_copy(part_ref, part_hbm, out_sems.at[SLOTS])
    copy.start()
    outs.append(copy)
    for copy in outs:
        copy.wait()


HBM = pl.BlockSpec(memory_space=pltpu.HBM)
SCALARS = pl.BlockSpec(memory_space=pltpu.SMEM)
VECTORS = pl.BlockSpec(memory_space=pltpu.VMEM)
CHUNK = (DEVICES, 16, 128)
ORDER = pltpu.VMEM((256, 512), BF16)
TABLE = pltpu.VMEM((2, 512, 512), BF16)
TURNS = pltpu.VMEM((16, 512), F32)
SPECTRAL = pltpu.VMEM((512, 512), F32)
BLOCK = (SLOTS, CELLS, 2, 384)
EDGE = (1, CELLS, 2, 384)
PARAMS = pltpu.CompilerParams(vmem_limit_bytes=VMEM_LIMIT)


def dma(count):
    return pltpu.SemaphoreType.DMA((count,))


def cost(flops, size):
    return pl.CostEstimate(flops=flops, bytes_accessed=size, transcendentals=0)


def forward(displacement, table, turns):
    shape = (8, 16, 16, 128)
    sent = pl.pallas_call(
        forward_kernel,
        in_specs=[HBM] * 4,
        out_specs=HBM,
        out_shape=jax.ShapeDtypeStruct(shape, F32),
        scratch_shapes=[
            pltpu.VMEM(BLOCK, F32), ORDER, TABLE, TURNS, pltpu.VMEM(shape, F32), SPECTRAL,
            dma(7), dma(4),
        ],
        compiler_params=PARAMS,
        cost_estimate=cost(10**9, 4 << 20),
    )(displacement, jnp.asarray(dof_order_table(1.0)), table, turns)
    return sent.reshape(CHUNK)


def middle(received, row_counts, table, turns, green_spectrum):
    shape = (DEVICES, 2, SLOTS, 2, 128)
    sent = pl.pallas_call(
        middle_kernel,
        in_specs=[SCALARS] + [HBM] * 4,
        out_specs=HBM,
        out_shape=jax.ShapeDtypeStruct(shape, F32),
        scratch_shapes=[
            pltpu.VMEM(shape, F32), TABLE, TURNS, pltpu.VMEM((32, PAD), F32),
            pltpu.VMEM(shape, F32), pltpu.VMEM((2, CELLS + 8, 2, 128), F32), SPECTRAL,
            dma(4), dma(4),
        ],
        compiler_params=PARAMS,
        cost_estimate=cost(3 * 10**9, 5 << 20),
    )(row_counts, received.reshape(shape), table, turns, green_spectrum)
    return sent.reshape(CHUNK)


def backward(received, structural, part, table, turns):
    return pl.pallas_call(
        backward_kernel,
        in_specs=[HBM] * 6,
        out_specs=HBM,
        out_shape=jax.ShapeDtypeStruct(BLOCK, F32),
        scratch_shapes=[
            pltpu.VMEM((8, 16, 16, 128), F32), pltpu.VMEM((SLOTS, 2, CELLS, 128), F32), ORDER, TABLE,
            TURNS,
            pltpu.VMEM((SLOTS, CELLS, 2, 128), F32), SPECTRAL, dma(5), dma(4),
        ],
        input_output_aliases={1: 0},
        compiler_params=PARAMS,
        cost_estimate=cost(10**9, 4 << 20),
    )(
        received.reshape(8, 16, 16, 128), structural, part,
        jnp.asarray(dof_order_table(1.0 / (PAD * PAD))), table, turns,
    )


def edge_rows(displacement, row_counts):
    return pl.pallas_call(
        edge_kernel,
        in_specs=[SCALARS, HBM],
        out_specs=[HBM] * 2,
        out_shape=[jax.ShapeDtypeStruct(EDGE, F32)] * 2,
        scratch_shapes=[pltpu.VMEM(EDGE, F32), pltpu.VMEM(EDGE, F32), dma(2), dma(2)],
        compiler_params=PARAMS,
        cost_estimate=cost(0, 3 << 20),
    )(row_counts, displacement)


def structure(
    displacement, above, below, stiffness, coupling, softening, biased, row_counts
):
    return pl.pallas_call(
        structural_kernel,
        in_specs=[SCALARS] + [HBM] * 4 + [VECTORS] * 3,
        out_specs=[HBM] * 2,
        out_shape=[
            jax.ShapeDtypeStruct(BLOCK, F32),
            jax.ShapeDtypeStruct((SLOTS, 2, CELLS, 128), F32),
        ],
        scratch_shapes=[
            pltpu.VMEM(BLOCK, F32), pltpu.VMEM(EDGE, F32), pltpu.VMEM(EDGE, F32),
            pltpu.VMEM((384, 384), BF16), pltpu.VMEM((SLOTS + 2, 2, CELLS, 384), F32),
            pltpu.VMEM((SLOTS, 2, CELLS, 128), F32), dma(7), dma(5),
        ],
        compiler_params=PARAMS,
        cost_estimate=cost(10**9, 8 << 20),
    )(row_counts, displacement, above, below, stiffness, coupling, softening, biased)


def per_device(
    displacement, stiffness, coupling, softening, electrode_mask, row_counts, green_spectrum
):
    table = jnp.asarray(dft_table())
    turns = jnp.asarray(twiddle_table())
    devices = lax.axis_size("row")
    up = [(i, i + 1) for i in range(devices - 1)]
    down = [(j, i) for i, j in up]
    first, last = edge_rows(displacement, row_counts)
    above = lax.ppermute(last, "row", up)
    below = lax.ppermute(first, "row", down)
    sent = forward(displacement, table, turns)
    sent, above, below = lax.optimization_barrier((sent, above, below))
    received = lax.all_to_all(sent, "row", split_axis=0, concat_axis=0, tiled=True)
    structural, part = structure(
        displacement, above, below, stiffness, coupling[None, :], softening[None, :],
        electrode_mask.astype(F32).T, row_counts,
    )
    received, structural, part = lax.optimization_barrier((received, structural, part))
    sent = middle(received, row_counts, table, turns, green_spectrum)
    received = lax.all_to_all(sent, "row", split_axis=0, concat_axis=0, tiled=True)
    return backward(received, structural, part, table, turns)


def solution(mesh):
    placed = (P("row", None, None, None), P(), P(), P(), P("row", None), P(), P("row", None))
    return jax.shard_map(
        per_device,
        mesh=mesh,
        in_specs=placed,
        out_specs=P("row", None, None, None),
        check_vma=False,
    )
```

```python
import math

import jax
import jax.numpy as jnp
import numpy as np
from jax import lax
from jax.experimental import pallas as pl
from jax.experimental.pallas import tpu as pltpu
from jax.sharding import PartitionSpec as P

CELL = 8
HALF = 512
CELLS = 256
PAD = 4096
SLOTS = 4
DEVICES = 128
VMEM_LIMIT = 60 * 1024 * 1024
F32 = jnp.float32
BF16 = jnp.bfloat16


def hi_lo_constant(values):
    values = np.asarray(values, np.float32)
    high = values.astype(jnp.bfloat16)
    low = (values - high.astype(np.float32)).astype(jnp.bfloat16)
    return np.stack([high, low])


def dft_table():
    cell = np.arange(CELLS)[:, None]
    freq = np.arange(HALF)[None, :]
    phase = (cell * freq % HALF) * (2.0 * math.pi / HALF)
    return hi_lo_constant(np.concatenate([np.cos(phase), np.sin(phase)], axis=0))


def twiddle_table():
    point = np.arange(CELL)[:, None]
    freq = np.arange(HALF)[None, :]
    phase = point * freq * (2.0 * math.pi / PAD)
    return np.concatenate([np.cos(phase), np.sin(phase)], axis=0).astype(np.float32)


def dof_order_table(scale):
    table = np.zeros((CELL, CELL // 2, SLOTS, 2, SLOTS, 128), np.float32)
    for b in range(CELL):
        for a in range(CELL):
            for slot in range(SLOTS):
                table[b, a // 2, slot, a % 2, slot, a * CELL + b] = scale
    return table.reshape(CELL * CELL * SLOTS, SLOTS * 128).astype(jnp.bfloat16)


def split(values):
    high = values.astype(BF16)
    return high, (values - high.astype(F32)).astype(BF16)


def dot(left, right):
    return jnp.dot(left, right, preferred_element_type=F32)


def dot_nt(left, right):
    return lax.dot_general(left, right, (((1,), (1,)), ((), ())), preferred_element_type=F32)


def dot3(left, right_ref):
    high, low = split(left)
    return dot(high, right_ref[0]) + (dot(high, right_ref[1]) + dot(low, right_ref[0]))


def dot3_nt(left_high, left_low, right):
    high, low = split(right)
    return dot_nt(left_high, high) + (dot_nt(left_high, low) + dot_nt(left_low, high))


ROOT = math.sqrt(0.5)


def cadd(x, y):
    return (x[0] + y[0], x[1] + y[1])


def csub(x, y):
    return (x[0] - y[0], x[1] - y[1])


def turn(x, eighths, sign):
    re, im = x
    if eighths == 0:
        return x
    if eighths == 2:
        return (-im, re) if sign > 0 else (im, -re)
    if eighths == 1:
        return ((re - im) * ROOT, (im + re) * ROOT) if sign > 0 else ((re + im) * ROOT, (im - re) * ROOT)
    return ((-re - im) * ROOT, (re - im) * ROOT) if sign > 0 else ((im - re) * ROOT, (-re - im) * ROOT)


def dft4(x, sign):
    s0, d0 = cadd(x[0], x[2]), csub(x[0], x[2])
    s1, d1 = cadd(x[1], x[3]), turn(csub(x[1], x[3]), 2, sign)
    return [cadd(s0, s1), cadd(d0, d1), csub(s0, s1), csub(d0, d1)]


def dft8(x, sign):
    even = dft4([cadd(x[n], x[n + 4]) for n in range(4)], sign)
    odd = dft4([turn(csub(x[n], x[n + 4]), n, sign) for n in range(4)], sign)
    return [v for pair in zip(even, odd) for v in pair]


def twist(x, cos, sin, sign):
    re, im = x
    if sign > 0:
        return (re * cos - im * sin, im * cos + re * sin)
    return (re * cos + im * sin, im * cos - re * sin)


def swap_groups(tiles, lane):
    low_half = lane < 64
    t0, t1, t2, t3 = tiles
    u0 = jnp.where(low_half, t0, pltpu.roll(t2, 64, 1))
    u2 = jnp.where(low_half, pltpu.roll(t0, 64, 1), t2)
    u1 = jnp.where(low_half, t1, pltpu.roll(t3, 64, 1))
    u3 = jnp.where(low_half, pltpu.roll(t1, 64, 1), t3)
    even = lax.rem(lane, 64) < 32
    return [
        jnp.where(even, u0, pltpu.roll(u1, 32, 1)),
        jnp.where(even, pltpu.roll(u0, 96, 1), u1),
        jnp.where(even, u2, pltpu.roll(u3, 32, 1)),
        jnp.where(even, pltpu.roll(u2, 96, 1), u3),
    ]


def tile(ref, part, block, row, lane_tile):
    start = part * 256 + block * 32 + row * 8
    return ref.at[start:start + 8, lane_tile * 128:lane_tile * 128 + 128]


def fetch(sources, targets, sems):
    copies = [
        pltpu.make_async_copy(source, target, sems.at[n])
        for n, (source, target) in enumerate(zip(sources, targets))
    ]
    for copy in copies:
        copy.start()
    return copies


def forward_kernel(
    counts_ref, x_hbm, order_hbm, table_hbm, twist_hbm, out_hbm, first_hbm, last_hbm,
    x_ref, order_ref, table_ref, twist_ref, out_ref, first_ref, last_ref, y_ref, sems, out_sems,
):
    count = counts_ref[lax.axis_index("row")]
    copies = fetch(
        (
            order_hbm, x_hbm.at[:, :, :, 0:128], table_hbm, twist_hbm,
            x_hbm.at[0:1], x_hbm.at[pl.ds(count - 1, 1)],
        ),
        (order_ref, x_ref, table_ref, twist_ref, first_ref, last_ref),
        sems,
    )
    copies[0].wait()
    copies[1].wait()
    planes = []
    for c in range(2):
        plane = jnp.concatenate([x_ref[slot, :, c, :] for slot in range(SLOTS)], axis=1)
        high, low = split(plane)
        planes.append(dot_nt(order_ref[...], high) + dot_nt(order_ref[...], low))
    w0, w1 = planes
    stacked = jnp.concatenate(
        [jnp.concatenate([w0, w1], axis=1), jnp.concatenate([w1, -w0], axis=1)], axis=0
    )
    copies[2].wait()
    y_ref[...] = dot3(stacked, table_ref)
    copies[3].wait()
    lane = lax.broadcasted_iota(jnp.int32, (64, 128), 1)
    outs = []
    for n, (held, target) in enumerate(((first_ref, first_hbm), (last_ref, last_hbm))):
        copies[4 + n].wait()
        copy = pltpu.make_async_copy(held, target, out_sems.at[4 + n])
        copy.start()
        outs.append(copy)
    for lane_tile in range(4):
        cut = slice(lane_tile * 128, lane_tile * 128 + 128)
        for row in range(4):
            points = []
            for b in range(CELL):
                value = tuple(tile(y_ref, o, b, row, lane_tile)[...] for o in range(2))
                if b:
                    value = twist(value, twist_ref[b:b + 1, cut], twist_ref[8 + b:9 + b, cut], -1)
                points.append(value)
            for k, value in enumerate(dft8(points, -1)):
                for o in range(2):
                    tile(y_ref, o, k, row, lane_tile)[...] = value[o]
        for o in range(2):
            block = y_ref[o * 256:o * 256 + 256, cut].reshape(8, 4, 8, 128)
            tiles = [block[:, row].reshape(64, 128) for row in range(4)]
            for u, value in enumerate(swap_groups(tiles, lane)):
                out_ref[:, lane_tile * 4 + u, o * 8:o * 8 + 8, :] = value.reshape(8, 8, 128)
        here = slice(lane_tile * 4, lane_tile * 4 + 4)
        copy = pltpu.make_async_copy(
            out_ref.at[:, here], out_hbm.at[:, here], out_sems.at[lane_tile]
        )
        copy.start()
        outs.append(copy)
    for copy in outs:
        copy.wait()


def middle_kernel(
    counts_ref, x_hbm, table_hbm, twist_hbm, green_hbm, out_hbm,
    x_ref, table_ref, twist_ref, green_ref, out_ref, cells_ref, y_ref, sems, out_sems,
):
    copies = fetch(
        (x_hbm, table_hbm, twist_hbm, green_hbm), (x_ref, table_ref, twist_ref, green_ref), sems
    )
    copies[0].wait()

    def gather(device, start):
        for c in range(2):
            cells_ref[c, pl.ds(start, SLOTS)] = x_ref[device, c]
        return start + counts_ref[device]

    lax.fori_loop(0, DEVICES, gather, 0, unroll=8)
    w = [
        jnp.concatenate([cells_ref[c, 0:CELLS, h, :].T for h in range(2)], axis=0)
        for c in range(2)
    ]
    stacked = jnp.concatenate(
        [jnp.concatenate([w[0], w[1]], axis=1), jnp.concatenate([w[1], -w[0]], axis=1)], axis=0
    )
    copies[1].wait()
    y_ref[...] = dot3(stacked, table_ref)
    copies[2].wait()
    copies[3].wait()
    for lane_tile in range(4):
        cut = slice(lane_tile * 128, lane_tile * 128 + 128)
        for row in range(4):
            points = []
            for a in range(CELL):
                block = (a % 2) * 4 + a // 2
                value = tuple(tile(y_ref, o, block, row, lane_tile)[...] for o in range(2))
                if a:
                    value = twist(value, twist_ref[a:a + 1, cut], twist_ref[8 + a:9 + a, cut], -1)
                points.append(value)
            spectrum = []
            for q, value in enumerate(dft8(points, -1)):
                first = q * 512 + lane_tile * 128
                green = green_ref[row * 8:row * 8 + 8, first:first + 128]
                spectrum.append((value[0] * green, value[1] * green))
            for a, value in enumerate(dft8(spectrum, 1)):
                block = (a % 2) * 4 + a // 2
                if a:
                    value = twist(value, twist_ref[a:a + 1, cut], twist_ref[8 + a:9 + a, cut], 1)
                for o in range(2):
                    tile(y_ref, o, block, row, lane_tile)[...] = value[o]
    back = inverse_cells(y_ref, table_ref)
    for c in range(2):
        cells_ref[c, CELLS:] = jnp.zeros((8, 2, 128), F32)
        for h in range(2):
            first = (c * 2 + h) * 128
            cells_ref[c, 0:CELLS, h, :] = back[:, first:first + 128]

    slot = lax.broadcasted_iota(jnp.int32, (SLOTS, 2, 128), 0)

    def scatter(device, start):
        count = counts_ref[device]
        for c in range(2):
            held = cells_ref[c, pl.ds(start, SLOTS)]
            out_ref[device, c] = jnp.where(slot < count, held, 0.0)
        return start + count

    outs = []
    start = 0
    for part in range(4):
        here = slice(part * 32, part * 32 + 32)
        start = lax.fori_loop(part * 32, part * 32 + 32, scatter, start, unroll=8)
        copy = pltpu.make_async_copy(out_ref.at[here], out_hbm.at[here], out_sems.at[part])
        copy.start()
        outs.append(copy)
    for copy in outs:
        copy.wait()


def inverse_cells(y_ref, table_ref):
    re, im = y_ref[0:256, :], y_ref[256:512, :]
    by_cos = jnp.concatenate([re, im], axis=0)
    by_sin = jnp.concatenate([-im, re], axis=0)
    return dot3_nt(table_ref[0, 0:256, :], table_ref[1, 0:256, :], by_cos) + dot3_nt(
        table_ref[0, 256:512, :], table_ref[1, 256:512, :], by_sin
    )


def backward_kernel(
    counts_ref, x_hbm, whole_hbm, part_hbm, above_hbm, below_hbm, couple_hbm, order_hbm,
    table_hbm, twist_hbm, out_hbm,
    x_ref, part_ref, above_ref, below_ref, couple_ref, first_ref, last_ref, order_ref,
    table_ref, twist_ref, out_ref, y_ref, sems, out_sems,
):
    count = counts_ref[lax.axis_index("row")]
    rest = slice(128, 384)
    first_row = whole_hbm.at[0, :, :, rest]
    last_row = whole_hbm.at[count - 1, :, :, rest]
    copies = fetch(
        (
            x_hbm, twist_hbm, table_hbm, order_hbm, part_hbm,
            above_hbm, below_hbm, couple_hbm, first_row, last_row,
        ),
        (
            x_ref, twist_ref, table_ref, order_ref, part_ref,
            above_ref, below_ref, couple_ref, first_ref, last_ref,
        ),
        sems,
    )
    lane = lax.broadcasted_iota(jnp.int32, (64, 128), 1)
    copies[0].wait()
    copies[1].wait()
    for lane_tile in range(4):
        cut = slice(lane_tile * 128, lane_tile * 128 + 128)
        for o in range(2):
            tiles = [
                x_ref[:, lane_tile * 4 + u, o * 8:o * 8 + 8, :].reshape(64, 128) for u in range(4)
            ]
            for row, value in enumerate(swap_groups(tiles, lane)):
                for k in range(CELL):
                    tile(y_ref, o, k, row, lane_tile)[...] = value[k * 8:k * 8 + 8, :]
        for row in range(4):
            points = [
                tuple(tile(y_ref, o, k, row, lane_tile)[...] for o in range(2))
                for k in range(CELL)
            ]
            for b, value in enumerate(dft8(points, 1)):
                if b:
                    value = twist(value, twist_ref[b:b + 1, cut], twist_ref[8 + b:9 + b, cut], 1)
                for o in range(2):
                    tile(y_ref, o, b, row, lane_tile)[...] = value[o]
    copies[2].wait()
    back = inverse_cells(y_ref, table_ref)
    copies[3].wait()
    for copy in copies[4:]:
        copy.wait()
    alone = count == 1
    couple = couple_ref[:, rest]
    last_ref[...] = last_ref[...] - couple * (
        below_ref[0, :, :, rest] + jnp.where(alone, above_ref[0, :, :, rest], 0.0)
    )
    last_copy = pltpu.make_async_copy(
        last_ref, out_hbm.at[count - 1, :, :, rest], out_sems.at[SLOTS]
    )
    last_copy.start()
    first_ref[...] = first_ref[...] - couple * (
        above_ref[0, :, :, rest] + jnp.where(alone, below_ref[0, :, :, rest], 0.0)
    )
    near = couple_ref[0:1, 0:128]
    halves = [split(back[:, c * 256:c * 256 + 256]) for c in range(2)]
    outs = []
    for slot in range(SLOTS):
        order = order_ref[:, slot * 128:slot * 128 + 128]
        for c in range(2):
            plane = dot(halves[c][0], order) + dot(halves[c][1], order)
            beside = jnp.where(slot == count - 1, below_ref[0, :, c, 0:128], 0.0)
            if slot == 0:
                beside = beside + above_ref[0, :, c, 0:128]
            out_ref[slot, :, c, :] = part_ref[slot, c] + plane - near * beside
        copy = pltpu.make_async_copy(
            out_ref.at[slot], out_hbm.at[slot, :, :, 0:128], out_sems.at[slot]
        )
        copy.start()
        outs.append(copy)
    last_copy.wait()
    copy = pltpu.make_async_copy(first_ref, out_hbm.at[0, :, :, rest], out_sems.at[SLOTS + 1])
    copy.start()
    outs.append(copy)
    for copy in outs:
        copy.wait()


def structural_kernel(
    counts_ref, x_hbm, stiff_hbm, couple_ref, soft_ref, mask_ref, out_hbm, part_hbm,
    x_ref, stiff_ref, plane_ref, part_ref, sems, out_sems,
):
    count = counts_ref[lax.axis_index("row")]
    copies = fetch(
        [stiff_hbm] + [x_hbm.at[slot] for slot in range(SLOTS)],
        [stiff_ref] + [x_ref.at[slot] for slot in range(SLOTS)],
        sems,
    )
    for slot in range(SLOTS):
        copies[1 + slot].wait()
        for c in range(2):
            plane_ref[slot + 1, c] = x_ref[slot, :, c, :]
    copies[0].wait()
    for c in range(2):
        plane_ref[0, c] = jnp.zeros((CELLS, 384), F32)
        plane_ref[count + 1, c] = jnp.zeros((CELLS, 384), F32)
    outs = []
    cell = lax.broadcasted_iota(jnp.int32, (CELLS, 1), 0)
    for slot in range(SLOTS):
        biased = mask_ref[:, slot:slot + 1]
        for c in range(2):
            own = plane_ref[slot + 1, c]
            elastic = dot(own.astype(BF16), stiff_ref[...])
            left = jnp.where(cell == 0, 0.0, pltpu.roll(own, 1, 0))
            right = jnp.where(cell == CELLS - 1, 0.0, pltpu.roll(own, CELLS - 1, 0))
            beside = plane_ref[slot, c] + plane_ref[slot + 2, c] + left + right
            value = elastic - couple_ref[...] * beside - (biased * soft_ref[...]) * own
            value = jnp.where(slot < count, value, 0.0)
            part_ref[slot, c] = value[:, 0:128]
            x_ref[slot, :, c, :] = value
        copy = pltpu.make_async_copy(x_ref.at[slot], out_hbm.at[slot], out_sems.at[slot])
        copy.start()
        outs.append(copy)
    copy = pltpu.make_async_copy(part_ref, part_hbm, out_sems.at[SLOTS])
    copy.start()
    outs.append(copy)
    for copy in outs:
        copy.wait()


HBM = pl.BlockSpec(memory_space=pltpu.HBM)
SCALARS = pl.BlockSpec(memory_space=pltpu.SMEM)
VECTORS = pl.BlockSpec(memory_space=pltpu.VMEM)
CHUNK = (DEVICES, 16, 128)
ORDER = pltpu.VMEM((256, 512), BF16)
TABLE = pltpu.VMEM((2, 512, 512), BF16)
TURNS = pltpu.VMEM((16, 512), F32)
SPECTRAL = pltpu.VMEM((512, 512), F32)
BLOCK = (SLOTS, CELLS, 2, 384)
EDGE = (1, CELLS, 2, 384)
PARAMS = pltpu.CompilerParams(vmem_limit_bytes=VMEM_LIMIT)


def dma(count):
    return pltpu.SemaphoreType.DMA((count,))


def cost(flops, size):
    return pl.CostEstimate(flops=flops, bytes_accessed=size, transcendentals=0)


def forward(displacement, row_counts, table, turns):
    shape = (8, 16, 16, 128)
    sent, first, last = pl.pallas_call(
        forward_kernel,
        in_specs=[SCALARS] + [HBM] * 4,
        out_specs=[HBM] * 3,
        out_shape=[
            jax.ShapeDtypeStruct(shape, F32),
            jax.ShapeDtypeStruct(EDGE, F32),
            jax.ShapeDtypeStruct(EDGE, F32),
        ],
        scratch_shapes=[
            pltpu.VMEM((SLOTS, CELLS, 2, 128), F32), ORDER, TABLE, TURNS, pltpu.VMEM(shape, F32),
            pltpu.VMEM(EDGE, F32), pltpu.VMEM(EDGE, F32), SPECTRAL, dma(6), dma(6),
        ],
        compiler_params=PARAMS,
        cost_estimate=cost(10**9, 7 << 20),
    )(row_counts, displacement, jnp.asarray(dof_order_table(1.0)), table, turns)
    return sent.reshape(CHUNK), first, last


def middle(received, row_counts, table, turns, green_spectrum):
    shape = (DEVICES, 2, SLOTS, 2, 128)
    sent = pl.pallas_call(
        middle_kernel,
        in_specs=[SCALARS] + [HBM] * 4,
        out_specs=HBM,
        out_shape=jax.ShapeDtypeStruct(shape, F32),
        scratch_shapes=[
            pltpu.VMEM(shape, F32), TABLE, TURNS, pltpu.VMEM((32, PAD), F32),
            pltpu.VMEM(shape, F32), pltpu.VMEM((2, CELLS + 8, 2, 128), F32), SPECTRAL,
            dma(4), dma(4),
        ],
        compiler_params=PARAMS,
        cost_estimate=cost(3 * 10**9, 5 << 20),
    )(row_counts, received.reshape(shape), table, turns, green_spectrum)
    return sent.reshape(CHUNK)


def backward(received, structural, part, above, below, coupling, row_counts, table, turns):
    edge = pltpu.VMEM((CELLS, 2, 256), F32)
    return pl.pallas_call(
        backward_kernel,
        in_specs=[SCALARS] + [HBM] * 9,
        out_specs=HBM,
        out_shape=jax.ShapeDtypeStruct(BLOCK, F32),
        scratch_shapes=[
            pltpu.VMEM((8, 16, 16, 128), F32), pltpu.VMEM((SLOTS, 2, CELLS, 128), F32),
            pltpu.VMEM(EDGE, F32), pltpu.VMEM(EDGE, F32), pltpu.VMEM((2, 384), F32), edge, edge,
            ORDER, TABLE, TURNS, pltpu.VMEM((SLOTS, CELLS, 2, 128), F32), SPECTRAL,
            dma(10), dma(SLOTS + 2),
        ],
        input_output_aliases={2: 0},
        compiler_params=PARAMS,
        cost_estimate=cost(10**9, 8 << 20),
    )(
        row_counts, received.reshape(8, 16, 16, 128), structural, part, above, below, coupling,
        jnp.asarray(dof_order_table(1.0 / (PAD * PAD))), table, turns,
    )


def structure(displacement, stiffness, coupling, softening, biased, row_counts):
    return pl.pallas_call(
        structural_kernel,
        in_specs=[SCALARS] + [HBM] * 2 + [VECTORS] * 3,
        out_specs=[HBM] * 2,
        out_shape=[
            jax.ShapeDtypeStruct(BLOCK, F32),
            jax.ShapeDtypeStruct((SLOTS, 2, CELLS, 128), F32),
        ],
        scratch_shapes=[
            pltpu.VMEM(BLOCK, F32), pltpu.VMEM((384, 384), BF16),
            pltpu.VMEM((SLOTS + 2, 2, CELLS, 384), F32),
            pltpu.VMEM((SLOTS, 2, CELLS, 128), F32), dma(5), dma(5),
        ],
        compiler_params=PARAMS,
        cost_estimate=cost(10**9, 8 << 20),
    )(row_counts, displacement, stiffness, coupling, softening, biased)


def per_device(
    displacement, stiffness, coupling, softening, electrode_mask, row_counts, green_spectrum
):
    table = jnp.asarray(dft_table())
    turns = jnp.asarray(twiddle_table())
    devices = lax.axis_size("row")
    up = [(i, i + 1) for i in range(devices - 1)]
    down = [(j, i) for i, j in up]
    sent, first, last = forward(displacement, row_counts, table, turns)
    above = lax.ppermute(last, "row", up)
    below = lax.ppermute(first, "row", down)
    received = lax.all_to_all(sent, "row", split_axis=0, concat_axis=0, tiled=True)
    couple = jnp.broadcast_to(coupling[None, :], (2, 384))
    structural, part = structure(
        displacement, stiffness, coupling[None, :], softening[None, :],
        electrode_mask.astype(F32).T, row_counts,
    )
    sent = middle(received, row_counts, table, turns, green_spectrum)
    received = lax.all_to_all(sent, "row", split_axis=0, concat_axis=0, tiled=True)
    return backward(received, structural, part, above, below, couple, row_counts, table, turns)


def solution(mesh):
    placed = (P("row", None, None, None), P(), P(), P(), P("row", None), P(), P("row", None))
    return jax.shard_map(
        per_device,
        mesh=mesh,
        in_specs=placed,
        out_specs=P("row", None, None, None),
        check_vma=False,
    )
```

```python
import math

import jax
import jax.numpy as jnp
import numpy as np
from jax import lax
from jax.experimental import pallas as pl
from jax.experimental.pallas import tpu as pltpu
from jax.sharding import PartitionSpec as P

CELL = 8
HALF = 512
CELLS = 256
PAD = 4096
SLOTS = 4
DEVICES = 128
VMEM_LIMIT = 60 * 1024 * 1024
F32 = jnp.float32
BF16 = jnp.bfloat16


def hi_lo_constant(values):
    values = np.asarray(values, np.float32)
    high = values.astype(jnp.bfloat16)
    low = (values - high.astype(np.float32)).astype(jnp.bfloat16)
    return np.stack([high, low])


def dft_table():
    cell = np.arange(CELLS)[:, None]
    freq = np.arange(HALF)[None, :]
    phase = (cell * freq % HALF) * (2.0 * math.pi / HALF)
    return hi_lo_constant(np.concatenate([np.cos(phase), np.sin(phase)], axis=0))


def twiddle_table():
    point = np.arange(CELL)[:, None]
    freq = np.arange(HALF)[None, :]
    phase = point * freq * (2.0 * math.pi / PAD)
    return np.concatenate([np.cos(phase), np.sin(phase)], axis=0).astype(np.float32)


def dof_order_table(scale):
    table = np.zeros((CELL, CELL // 2, SLOTS, 2, SLOTS, 128), np.float32)
    for b in range(CELL):
        for a in range(CELL):
            for slot in range(SLOTS):
                table[b, a // 2, slot, a % 2, slot, a * CELL + b] = scale
    return table.reshape(CELL * CELL * SLOTS, SLOTS * 128).astype(jnp.bfloat16)


def split(values):
    high = values.astype(BF16)
    return high, (values - high.astype(F32)).astype(BF16)


def dot(left, right):
    return jnp.dot(left, right, preferred_element_type=F32)


def dot_nt(left, right):
    return lax.dot_general(left, right, (((1,), (1,)), ((), ())), preferred_element_type=F32)


def dot3(left, right_ref):
    high, low = split(left)
    return dot(high, right_ref[0]) + (dot(high, right_ref[1]) + dot(low, right_ref[0]))


def dot3_nt(left_high, left_low, right):
    high, low = split(right)
    return dot_nt(left_high, high) + (dot_nt(left_high, low) + dot_nt(left_low, high))


ROOT = math.sqrt(0.5)


def cadd(x, y):
    return (x[0] + y[0], x[1] + y[1])


def csub(x, y):
    return (x[0] - y[0], x[1] - y[1])


def turn(x, eighths, sign):
    re, im = x
    if eighths == 0:
        return x
    if eighths == 2:
        return (-im, re) if sign > 0 else (im, -re)
    if eighths == 1:
        return ((re - im) * ROOT, (im + re) * ROOT) if sign > 0 else ((re + im) * ROOT, (im - re) * ROOT)
    return ((-re - im) * ROOT, (re - im) * ROOT) if sign > 0 else ((im - re) * ROOT, (-re - im) * ROOT)


def dft4(x, sign):
    s0, d0 = cadd(x[0], x[2]), csub(x[0], x[2])
    s1, d1 = cadd(x[1], x[3]), turn(csub(x[1], x[3]), 2, sign)
    return [cadd(s0, s1), cadd(d0, d1), csub(s0, s1), csub(d0, d1)]


def dft8(x, sign):
    even = dft4([cadd(x[n], x[n + 4]) for n in range(4)], sign)
    odd = dft4([turn(csub(x[n], x[n + 4]), n, sign) for n in range(4)], sign)
    return [v for pair in zip(even, odd) for v in pair]


def twist(x, cos, sin, sign):
    re, im = x
    if sign > 0:
        return (re * cos - im * sin, im * cos + re * sin)
    return (re * cos + im * sin, im * cos - re * sin)


def swap_groups(tiles, lane):
    low_half = lane < 64
    t0, t1, t2, t3 = tiles
    u0 = jnp.where(low_half, t0, pltpu.roll(t2, 64, 1))
    u2 = jnp.where(low_half, pltpu.roll(t0, 64, 1), t2)
    u1 = jnp.where(low_half, t1, pltpu.roll(t3, 64, 1))
    u3 = jnp.where(low_half, pltpu.roll(t1, 64, 1), t3)
    even = lax.rem(lane, 64) < 32
    return [
        jnp.where(even, u0, pltpu.roll(u1, 32, 1)),
        jnp.where(even, pltpu.roll(u0, 96, 1), u1),
        jnp.where(even, u2, pltpu.roll(u3, 32, 1)),
        jnp.where(even, pltpu.roll(u2, 96, 1), u3),
    ]


def tile(ref, part, block, row, lane_tile):
    start = part * 256 + block * 32 + row * 8
    return ref.at[start:start + 8, lane_tile * 128:lane_tile * 128 + 128]


def fetch(sources, targets, sems):
    copies = [
        pltpu.make_async_copy(source, target, sems.at[n])
        for n, (source, target) in enumerate(zip(sources, targets))
    ]
    for copy in copies:
        copy.start()
    return copies


def forward_kernel(
    counts_hbm, x_hbm, order_hbm, table_hbm, twist_hbm, out_hbm, first_hbm, last_hbm,
    counts_ref, x_ref, order_ref, table_ref, twist_ref, out_ref, first_ref, last_ref, y_ref,
    sems, out_sems,
):
    copies = fetch(
        (
            counts_hbm, x_hbm.at[:, :, :, 0:128], order_hbm, table_hbm, twist_hbm,
            x_hbm.at[0:1],
        ),
        (counts_ref, x_ref, order_ref, table_ref, twist_ref, first_ref),
        sems,
    )
    copies[0].wait()
    count = counts_ref[lax.axis_index("row")]
    copies += fetch((x_hbm.at[pl.ds(count - 1, 1)],), (last_ref,), sems.at[pl.ds(6, 1)])
    copies[1].wait()
    copies[2].wait()
    planes = []
    for c in range(2):
        plane = jnp.concatenate([x_ref[slot, :, c, :] for slot in range(SLOTS)], axis=1)
        high, low = split(plane)
        planes.append(dot_nt(order_ref[...], high) + dot_nt(order_ref[...], low))
    w0, w1 = planes
    stacked = jnp.concatenate(
        [jnp.concatenate([w0, w1], axis=1), jnp.concatenate([w1, -w0], axis=1)], axis=0
    )
    copies[3].wait()
    for cut in (slice(0, 256), slice(256, 512)):
        y_ref[:, cut] = dot3(stacked, table_ref.at[:, :, cut])
    copies[4].wait()
    lane = lax.broadcasted_iota(jnp.int32, (64, 128), 1)
    outs = []
    for n, (held, target) in enumerate(((first_ref, first_hbm), (last_ref, last_hbm))):
        copies[5 + n].wait()
        copy = pltpu.make_async_copy(held, target, out_sems.at[4 + n])
        copy.start()
        outs.append(copy)
    for lane_tile in range(4):
        cut = slice(lane_tile * 128, lane_tile * 128 + 128)
        for row in range(4):
            points = []
            for b in range(CELL):
                value = tuple(tile(y_ref, o, b, row, lane_tile)[...] for o in range(2))
                if b:
                    value = twist(value, twist_ref[b:b + 1, cut], twist_ref[8 + b:9 + b, cut], -1)
                points.append(value)
            for k, value in enumerate(dft8(points, -1)):
                for o in range(2):
                    tile(y_ref, o, k, row, lane_tile)[...] = value[o]
        for o in range(2):
            block = y_ref[o * 256:o * 256 + 256, cut].reshape(8, 4, 8, 128)
            tiles = [block[:, row].reshape(64, 128) for row in range(4)]
            for u, value in enumerate(swap_groups(tiles, lane)):
                out_ref[:, lane_tile * 4 + u, o * 8:o * 8 + 8, :] = value.reshape(8, 8, 128)
        here = slice(lane_tile * 4, lane_tile * 4 + 4)
        copy = pltpu.make_async_copy(
            out_ref.at[:, here], out_hbm.at[:, here], out_sems.at[lane_tile]
        )
        copy.start()
        outs.append(copy)
    for copy in outs:
        copy.wait()


def middle_kernel(
    counts_hbm, x_hbm, table_hbm, twist_hbm, green_hbm, out_hbm,
    counts_ref, x_ref, table_ref, twist_ref, green_ref, out_ref, cells_ref, y_ref, sems, out_sems,
):
    copies = fetch(
        (x_hbm, table_hbm, twist_hbm, green_hbm, counts_hbm),
        (x_ref, table_ref, twist_ref, green_ref, counts_ref),
        sems,
    )
    copies[4].wait()
    copies[0].wait()

    def gather(device, start):
        for c in range(2):
            cells_ref[c, pl.ds(start, SLOTS)] = x_ref[device, c]
        return start + counts_ref[device]

    lax.fori_loop(0, DEVICES, gather, 0, unroll=8)
    w = [
        jnp.concatenate([cells_ref[c, 0:CELLS, h, :].T for h in range(2)], axis=0)
        for c in range(2)
    ]
    stacked = jnp.concatenate(
        [jnp.concatenate([w[0], w[1]], axis=1), jnp.concatenate([w[1], -w[0]], axis=1)], axis=0
    )
    copies[1].wait()
    for cut in (slice(0, 256), slice(256, 512)):
        y_ref[:, cut] = dot3(stacked, table_ref.at[:, :, cut])
    copies[2].wait()
    copies[3].wait()
    back = 0.0
    for lane_tile in range(4):
        cut = slice(lane_tile * 128, lane_tile * 128 + 128)
        for row in range(4):
            points = []
            for a in range(CELL):
                block = (a % 2) * 4 + a // 2
                value = tuple(tile(y_ref, o, block, row, lane_tile)[...] for o in range(2))
                if a:
                    value = twist(value, twist_ref[a:a + 1, cut], twist_ref[8 + a:9 + a, cut], -1)
                points.append(value)
            spectrum = []
            for q, value in enumerate(dft8(points, -1)):
                first = q * 512 + lane_tile * 128
                green = green_ref[row * 8:row * 8 + 8, first:first + 128]
                spectrum.append((value[0] * green, value[1] * green))
            for a, value in enumerate(dft8(spectrum, 1)):
                block = (a % 2) * 4 + a // 2
                if a:
                    value = twist(value, twist_ref[a:a + 1, cut], twist_ref[8 + a:9 + a, cut], 1)
                for o in range(2):
                    tile(y_ref, o, block, row, lane_tile)[...] = value[o]
        if lane_tile % 2:
            half = slice(lane_tile * 128 - 128, lane_tile * 128 + 128)
            back = back + inverse_cells(y_ref, table_ref, half)
    for c in range(2):
        cells_ref[c, CELLS:] = jnp.zeros((8, 2, 128), F32)
        for h in range(2):
            first = (c * 2 + h) * 128
            cells_ref[c, 0:CELLS, h, :] = back[:, first:first + 128]

    slot = lax.broadcasted_iota(jnp.int32, (SLOTS, 2, 128), 0)

    def scatter(device, start):
        count = counts_ref[device]
        for c in range(2):
            held = cells_ref[c, pl.ds(start, SLOTS)]
            out_ref[device, c] = jnp.where(slot < count, held, 0.0)
        return start + count

    outs = []
    start = 0
    for part in range(4):
        here = slice(part * 32, part * 32 + 32)
        start = lax.fori_loop(part * 32, part * 32 + 32, scatter, start, unroll=8)
        copy = pltpu.make_async_copy(out_ref.at[here], out_hbm.at[here], out_sems.at[part])
        copy.start()
        outs.append(copy)
    for copy in outs:
        copy.wait()


def inverse_cells(y_ref, table_ref, cut):
    re, im = y_ref[0:256, cut], y_ref[256:512, cut]
    by_cos = jnp.concatenate([re, im], axis=0)
    by_sin = jnp.concatenate([-im, re], axis=0)
    return dot3_nt(table_ref[0, 0:256, cut], table_ref[1, 0:256, cut], by_cos) + dot3_nt(
        table_ref[0, 256:512, cut], table_ref[1, 256:512, cut], by_sin
    )


def backward_kernel(
    counts_hbm, x_hbm, whole_hbm, part_hbm, above_hbm, below_hbm, couple_hbm, order_hbm,
    table_hbm, twist_hbm, out_hbm,
    counts_ref, x_ref, part_ref, above_ref, below_ref, couple_ref, first_ref, last_ref, order_ref,
    table_ref, twist_ref, out_ref, y_ref, sems, out_sems,
):
    rest = slice(128, 384)
    first_row = whole_hbm.at[0, :, :, rest]
    copies = fetch(
        (
            x_hbm, twist_hbm, table_hbm, order_hbm, part_hbm,
            above_hbm, below_hbm, couple_hbm, first_row, counts_hbm,
        ),
        (
            x_ref, twist_ref, table_ref, order_ref, part_ref,
            above_ref, below_ref, couple_ref, first_ref, counts_ref,
        ),
        sems,
    )
    copies.pop().wait()
    count = counts_ref[lax.axis_index("row")]
    copies += fetch(
        (whole_hbm.at[count - 1, :, :, rest],), (last_ref,), sems.at[pl.ds(10, 1)]
    )
    lane = lax.broadcasted_iota(jnp.int32, (64, 128), 1)
    copies[0].wait()
    copies[1].wait()
    copies[2].wait()
    back = 0.0
    for lane_tile in range(4):
        cut = slice(lane_tile * 128, lane_tile * 128 + 128)
        for o in range(2):
            tiles = [
                x_ref[:, lane_tile * 4 + u, o * 8:o * 8 + 8, :].reshape(64, 128) for u in range(4)
            ]
            for row, value in enumerate(swap_groups(tiles, lane)):
                for k in range(CELL):
                    tile(y_ref, o, k, row, lane_tile)[...] = value[k * 8:k * 8 + 8, :]
        for row in range(4):
            points = [
                tuple(tile(y_ref, o, k, row, lane_tile)[...] for o in range(2))
                for k in range(CELL)
            ]
            for b, value in enumerate(dft8(points, 1)):
                if b:
                    value = twist(value, twist_ref[b:b + 1, cut], twist_ref[8 + b:9 + b, cut], 1)
                for o in range(2):
                    tile(y_ref, o, b, row, lane_tile)[...] = value[o]
        if lane_tile % 2:
            half = slice(lane_tile * 128 - 128, lane_tile * 128 + 128)
            back = back + inverse_cells(y_ref, table_ref, half)
    copies[3].wait()
    for copy in copies[4:]:
        copy.wait()
    alone = count == 1
    couple = couple_ref[:, rest]
    last_ref[...] = last_ref[...] - couple * (
        below_ref[0, :, :, rest] + jnp.where(alone, above_ref[0, :, :, rest], 0.0)
    )
    last_copy = pltpu.make_async_copy(
        last_ref, out_hbm.at[count - 1, :, :, rest], out_sems.at[SLOTS]
    )
    last_copy.start()
    first_ref[...] = first_ref[...] - couple * (
        above_ref[0, :, :, rest] + jnp.where(alone, below_ref[0, :, :, rest], 0.0)
    )
    near = couple_ref[0:1, 0:128]
    halves = [split(back[:, c * 256:c * 256 + 256]) for c in range(2)]
    outs = []
    for slot in range(SLOTS):
        order = order_ref[:, slot * 128:slot * 128 + 128]
        for c in range(2):
            plane = dot(halves[c][0], order) + dot(halves[c][1], order)
            beside = jnp.where(slot == count - 1, below_ref[0, :, c, 0:128], 0.0)
            if slot == 0:
                beside = beside + above_ref[0, :, c, 0:128]
            out_ref[slot, :, c, :] = part_ref[slot, c] + plane - near * beside
        copy = pltpu.make_async_copy(
            out_ref.at[slot], out_hbm.at[slot, :, :, 0:128], out_sems.at[slot]
        )
        copy.start()
        outs.append(copy)
        if slot == 1:
            last_copy.wait()
            copy = pltpu.make_async_copy(
                first_ref, out_hbm.at[0, :, :, rest], out_sems.at[SLOTS + 1]
            )
            copy.start()
            outs.append(copy)
    for copy in outs:
        copy.wait()


def structural_kernel(
    counts_ref, x_hbm, stiff_hbm, couple_ref, soft_ref, mask_ref, out_hbm, part_hbm,
    x_ref, stiff_ref, plane_ref, part_ref, sems, out_sems,
):
    count = counts_ref[lax.axis_index("row")]
    copies = fetch(
        [stiff_hbm] + [x_hbm.at[slot] for slot in range(SLOTS)],
        [stiff_ref] + [x_ref.at[slot] for slot in range(SLOTS)],
        sems,
    )
    for slot in range(SLOTS):
        copies[1 + slot].wait()
        for c in range(2):
            plane_ref[slot + 1, c] = x_ref[slot, :, c, :]
    copies[0].wait()
    for c in range(2):
        plane_ref[0, c] = jnp.zeros((CELLS, 384), F32)
        plane_ref[count + 1, c] = jnp.zeros((CELLS, 384), F32)
    outs = []
    cell = lax.broadcasted_iota(jnp.int32, (CELLS, 1), 0)
    for slot in range(SLOTS):
        biased = mask_ref[:, slot:slot + 1]
        for c in range(2):
            own = plane_ref[slot + 1, c]
            elastic = dot(own.astype(BF16), stiff_ref[...])
            left = jnp.where(cell == 0, 0.0, pltpu.roll(own, 1, 0))
            right = jnp.where(cell == CELLS - 1, 0.0, pltpu.roll(own, CELLS - 1, 0))
            beside = plane_ref[slot, c] + plane_ref[slot + 2, c] + left + right
            value = elastic - couple_ref[...] * beside - (biased * soft_ref[...]) * own
            value = jnp.where(slot < count, value, 0.0)
            part_ref[slot, c] = value[:, 0:128]
            x_ref[slot, :, c, :] = value
        copy = pltpu.make_async_copy(x_ref.at[slot], out_hbm.at[slot], out_sems.at[slot])
        copy.start()
        outs.append(copy)
    copy = pltpu.make_async_copy(part_ref, part_hbm, out_sems.at[SLOTS])
    copy.start()
    outs.append(copy)
    for copy in outs:
        copy.wait()


HBM = pl.BlockSpec(memory_space=pltpu.HBM)
SCALARS = pl.BlockSpec(memory_space=pltpu.SMEM)
VECTORS = pl.BlockSpec(memory_space=pltpu.VMEM)
CHUNK = (DEVICES, 16, 128)
COUNTS = pltpu.SMEM((DEVICES,), jnp.int32)
ORDER = pltpu.VMEM((256, 512), BF16)
TABLE = pltpu.VMEM((2, 512, 512), BF16)
TURNS = pltpu.VMEM((16, 512), F32)
SPECTRAL = pltpu.VMEM((512, 512), F32)
BLOCK = (SLOTS, CELLS, 2, 384)
EDGE = (1, CELLS, 2, 384)
PARAMS = pltpu.CompilerParams(vmem_limit_bytes=VMEM_LIMIT)


def dma(count):
    return pltpu.SemaphoreType.DMA((count,))


def cost(flops, size):
    return pl.CostEstimate(flops=flops, bytes_accessed=size, transcendentals=0)


def forward(displacement, row_counts, table, turns):
    shape = (8, 16, 16, 128)
    sent, first, last = pl.pallas_call(
        forward_kernel,
        in_specs=[HBM] * 5,
        out_specs=[HBM] * 3,
        out_shape=[
            jax.ShapeDtypeStruct(shape, F32),
            jax.ShapeDtypeStruct(EDGE, F32),
            jax.ShapeDtypeStruct(EDGE, F32),
        ],
        scratch_shapes=[
            COUNTS, pltpu.VMEM((SLOTS, CELLS, 2, 128), F32), ORDER, TABLE, TURNS,
            pltpu.VMEM(shape, F32),
            pltpu.VMEM(EDGE, F32), pltpu.VMEM(EDGE, F32), SPECTRAL, dma(7), dma(6),
        ],
        compiler_params=PARAMS,
        cost_estimate=cost(10**9, 7 << 20),
    )(row_counts, displacement, jnp.asarray(dof_order_table(1.0)), table, turns)
    return sent.reshape(CHUNK), first, last


def middle(received, row_counts, table, turns, green_spectrum):
    shape = (DEVICES, 2, SLOTS, 2, 128)
    sent = pl.pallas_call(
        middle_kernel,
        in_specs=[HBM] * 5,
        out_specs=HBM,
        out_shape=jax.ShapeDtypeStruct(shape, F32),
        scratch_shapes=[
            COUNTS, pltpu.VMEM(shape, F32), TABLE, TURNS, pltpu.VMEM((32, PAD), F32),
            pltpu.VMEM(shape, F32), pltpu.VMEM((2, CELLS + 8, 2, 128), F32), SPECTRAL,
            dma(5), dma(4),
        ],
        compiler_params=PARAMS,
        cost_estimate=cost(3 * 10**9, 5 << 20),
    )(row_counts, received.reshape(shape), table, turns, green_spectrum)
    return sent.reshape(CHUNK)


def backward(received, structural, part, above, below, coupling, row_counts, table, turns):
    edge = pltpu.VMEM((CELLS, 2, 256), F32)
    return pl.pallas_call(
        backward_kernel,
        in_specs=[HBM] * 10,
        out_specs=HBM,
        out_shape=jax.ShapeDtypeStruct(BLOCK, F32),
        scratch_shapes=[
            COUNTS, pltpu.VMEM((8, 16, 16, 128), F32), pltpu.VMEM((SLOTS, 2, CELLS, 128), F32),
            pltpu.VMEM(EDGE, F32), pltpu.VMEM(EDGE, F32), pltpu.VMEM((2, 384), F32), edge, edge,
            ORDER, TABLE, TURNS, pltpu.VMEM((SLOTS, CELLS, 2, 128), F32), SPECTRAL,
            dma(11), dma(SLOTS + 2),
        ],
        input_output_aliases={2: 0},
        compiler_params=PARAMS,
        cost_estimate=cost(10**9, 8 << 20),
    )(
        row_counts, received.reshape(8, 16, 16, 128), structural, part, above, below, coupling,
        jnp.asarray(dof_order_table(1.0 / (PAD * PAD))), table, turns,
    )


def structure(displacement, stiffness, coupling, softening, biased, row_counts):
    return pl.pallas_call(
        structural_kernel,
        in_specs=[SCALARS] + [HBM] * 2 + [VECTORS] * 3,
        out_specs=[HBM] * 2,
        out_shape=[
            jax.ShapeDtypeStruct(BLOCK, F32),
            jax.ShapeDtypeStruct((SLOTS, 2, CELLS, 128), F32),
        ],
        scratch_shapes=[
            pltpu.VMEM(BLOCK, F32), pltpu.VMEM((384, 384), BF16),
            pltpu.VMEM((SLOTS + 2, 2, CELLS, 384), F32),
            pltpu.VMEM((SLOTS, 2, CELLS, 128), F32), dma(5), dma(5),
        ],
        compiler_params=PARAMS,
        cost_estimate=cost(10**9, 8 << 20),
    )(row_counts, displacement, stiffness, coupling, softening, biased)


def per_device(
    displacement, stiffness, coupling, softening, electrode_mask, row_counts, green_spectrum
):
    table = jnp.asarray(dft_table())
    turns = jnp.asarray(twiddle_table())
    devices = lax.axis_size("row")
    up = [(i, i + 1) for i in range(devices - 1)]
    down = [(j, i) for i, j in up]
    sent, first, last = forward(displacement, row_counts, table, turns)
    above = lax.ppermute(last, "row", up)
    below = lax.ppermute(first, "row", down)
    received = lax.all_to_all(sent, "row", split_axis=0, concat_axis=0, tiled=True)
    couple = jnp.broadcast_to(coupling[None, :], (2, 384))
    structural, part = structure(
        displacement, stiffness, coupling[None, :], softening[None, :],
        electrode_mask.astype(F32).T, row_counts,
    )
    sent = middle(received, row_counts, table, turns, green_spectrum)
    received = lax.all_to_all(sent, "row", split_axis=0, concat_axis=0, tiled=True)
    return backward(received, structural, part, above, below, couple, row_counts, table, turns)


def solution(mesh):
    placed = (P("row", None, None, None), P(), P(), P(), P("row", None), P(), P("row", None))
    return jax.shard_map(
        per_device,
        mesh=mesh,
        in_specs=placed,
        out_specs=P("row", None, None, None),
        check_vma=False,
    )
```

```python
import math

import jax
import jax.numpy as jnp
import numpy as np
from jax import lax
from jax.experimental import pallas as pl
from jax.experimental.pallas import tpu as pltpu
from jax.sharding import PartitionSpec as P

CELL = 8
HALF = 512
CELLS = 256
PAD = 4096
SLOTS = 4
DEVICES = 128
VMEM_LIMIT = 60 * 1024 * 1024
F32 = jnp.float32
BF16 = jnp.bfloat16


def hi_lo_constant(values):
    values = np.asarray(values, np.float32)
    high = values.astype(jnp.bfloat16)
    low = (values - high.astype(np.float32)).astype(jnp.bfloat16)
    return np.stack([high, low])


def dft_table():
    cell = np.arange(CELLS)[:, None]
    freq = np.arange(HALF)[None, :]
    phase = (cell * freq % HALF) * (2.0 * math.pi / HALF)
    return hi_lo_constant(np.concatenate([np.cos(phase), np.sin(phase)], axis=0))


def twiddle_table():
    point = np.arange(CELL)[:, None]
    freq = np.arange(HALF)[None, :]
    phase = point * freq * (2.0 * math.pi / PAD)
    return np.concatenate([np.cos(phase), np.sin(phase)], axis=0).astype(np.float32)


def dof_order_table(scale):
    table = np.zeros((CELL, CELL // 2, SLOTS, 2, SLOTS, 128), np.float32)
    for b in range(CELL):
        for a in range(CELL):
            for slot in range(SLOTS):
                table[b, a // 2, slot, a % 2, slot, a * CELL + b] = scale
    return table.reshape(CELL * CELL * SLOTS, SLOTS * 128).astype(jnp.bfloat16)


def split(values):
    high = values.astype(BF16)
    return high, (values - high.astype(F32)).astype(BF16)


def dot(left, right):
    return jnp.dot(left, right, preferred_element_type=F32)


def dot_nt(left, right):
    return lax.dot_general(left, right, (((1,), (1,)), ((), ())), preferred_element_type=F32)


def dot3(left, right_ref):
    high, low = split(left)
    return dot(high, right_ref[0]) + (dot(high, right_ref[1]) + dot(low, right_ref[0]))


def dot3_nt(left_high, left_low, right):
    high, low = split(right)
    return dot_nt(left_high, high) + (dot_nt(left_high, low) + dot_nt(left_low, high))


ROOT = math.sqrt(0.5)


def cadd(x, y):
    return (x[0] + y[0], x[1] + y[1])


def csub(x, y):
    return (x[0] - y[0], x[1] - y[1])


def turn(x, eighths, sign):
    re, im = x
    if eighths == 0:
        return x
    if eighths == 2:
        return (-im, re) if sign > 0 else (im, -re)
    if eighths == 1:
        return ((re - im) * ROOT, (im + re) * ROOT) if sign > 0 else ((re + im) * ROOT, (im - re) * ROOT)
    return ((-re - im) * ROOT, (re - im) * ROOT) if sign > 0 else ((im - re) * ROOT, (-re - im) * ROOT)


def dft4(x, sign):
    s0, d0 = cadd(x[0], x[2]), csub(x[0], x[2])
    s1, d1 = cadd(x[1], x[3]), turn(csub(x[1], x[3]), 2, sign)
    return [cadd(s0, s1), cadd(d0, d1), csub(s0, s1), csub(d0, d1)]


def dft8(x, sign):
    even = dft4([cadd(x[n], x[n + 4]) for n in range(4)], sign)
    odd = dft4([turn(csub(x[n], x[n + 4]), n, sign) for n in range(4)], sign)
    return [v for pair in zip(even, odd) for v in pair]


def twist(x, cos, sin, sign):
    re, im = x
    if sign > 0:
        return (re * cos - im * sin, im * cos + re * sin)
    return (re * cos + im * sin, im * cos - re * sin)


def swap_groups(tiles, lane):
    low_half = lane < 64
    t0, t1, t2, t3 = tiles
    u0 = jnp.where(low_half, t0, pltpu.roll(t2, 64, 1))
    u2 = jnp.where(low_half, pltpu.roll(t0, 64, 1), t2)
    u1 = jnp.where(low_half, t1, pltpu.roll(t3, 64, 1))
    u3 = jnp.where(low_half, pltpu.roll(t1, 64, 1), t3)
    even = lax.rem(lane, 64) < 32
    return [
        jnp.where(even, u0, pltpu.roll(u1, 32, 1)),
        jnp.where(even, pltpu.roll(u0, 96, 1), u1),
        jnp.where(even, u2, pltpu.roll(u3, 32, 1)),
        jnp.where(even, pltpu.roll(u2, 96, 1), u3),
    ]


def tile(ref, part, block, row, lane_tile):
    start = part * 256 + block * 32 + row * 8
    return ref.at[start:start + 8, lane_tile * 128:lane_tile * 128 + 128]


def fetch(sources, targets, sems):
    copies = [
        pltpu.make_async_copy(source, target, sems.at[n])
        for n, (source, target) in enumerate(zip(sources, targets))
    ]
    for copy in copies:
        copy.start()
    return copies


def forward_kernel(
    counts_hbm, x_hbm, order_hbm, table_hbm, twist_hbm, out_hbm, first_hbm, last_hbm,
    counts_ref, x_ref, order_ref, table_ref, twist_ref, out_ref, first_ref, last_ref, y_ref,
    sems, out_sems,
):
    copies = fetch(
        (
            counts_hbm, x_hbm.at[:, :, :, 0:128], order_hbm, table_hbm, twist_hbm,
            x_hbm.at[0:1],
        ),
        (counts_ref, x_ref, order_ref, table_ref, twist_ref, first_ref),
        sems,
    )
    copies[0].wait()
    count = counts_ref[lax.axis_index("row")]
    copies += fetch((x_hbm.at[pl.ds(count - 1, 1)],), (last_ref,), sems.at[pl.ds(6, 1)])
    copies[1].wait()
    copies[2].wait()
    planes = []
    for c in range(2):
        plane = jnp.concatenate([x_ref[slot, :, c, :] for slot in range(SLOTS)], axis=1)
        high, low = split(plane)
        planes.append(dot_nt(order_ref[...], high) + dot_nt(order_ref[...], low))
    w0, w1 = planes
    stacked = jnp.concatenate(
        [jnp.concatenate([w0, w1], axis=1), jnp.concatenate([w1, -w0], axis=1)], axis=0
    )
    copies[3].wait()
    for cut in (slice(0, 256), slice(256, 512)):
        y_ref[:, cut] = dot3(stacked, table_ref.at[:, :, cut])
    copies[4].wait()
    lane = lax.broadcasted_iota(jnp.int32, (64, 128), 1)
    outs = []
    for n, (held, target) in enumerate(((first_ref, first_hbm), (last_ref, last_hbm))):
        copies[5 + n].wait()
        copy = pltpu.make_async_copy(held, target, out_sems.at[4 + n])
        copy.start()
        outs.append(copy)
    for lane_tile in range(4):
        cut = slice(lane_tile * 128, lane_tile * 128 + 128)
        for row in range(4):
            points = []
            for b in range(CELL):
                value = tuple(tile(y_ref, o, b, row, lane_tile)[...] for o in range(2))
                if b:
                    value = twist(value, twist_ref[b:b + 1, cut], twist_ref[8 + b:9 + b, cut], -1)
                points.append(value)
            for k, value in enumerate(dft8(points, -1)):
                for o in range(2):
                    tile(y_ref, o, k, row, lane_tile)[...] = value[o]
        for o in range(2):
            block = y_ref[o * 256:o * 256 + 256, cut].reshape(8, 4, 8, 128)
            tiles = [block[:, row].reshape(64, 128) for row in range(4)]
            for u, value in enumerate(swap_groups(tiles, lane)):
                out_ref[:, lane_tile * 4 + u, o * 8:o * 8 + 8, :] = value.reshape(8, 8, 128)
        here = slice(lane_tile * 4, lane_tile * 4 + 4)
        copy = pltpu.make_async_copy(
            out_ref.at[:, here], out_hbm.at[:, here], out_sems.at[lane_tile]
        )
        copy.start()
        outs.append(copy)
    for copy in outs:
        copy.wait()


def middle_kernel(
    counts_hbm, x_ref, table_hbm, twist_hbm, green_hbm, out_hbm,
    counts_ref, table_ref, twist_ref, green_ref, out_ref, cells_ref, y_ref, sems, out_sems,
):
    copies = fetch(
        (table_hbm, twist_hbm, green_hbm, counts_hbm),
        (table_ref, twist_ref, green_ref, counts_ref),
        sems,
    )
    copies[3].wait()

    def gather(device, start):
        for c in range(2):
            cells_ref[c, pl.ds(start, SLOTS)] = x_ref[device, c]
        return start + counts_ref[device]

    lax.fori_loop(0, DEVICES, gather, 0, unroll=8)
    w = [
        jnp.concatenate([cells_ref[c, 0:CELLS, h, :].T for h in range(2)], axis=0)
        for c in range(2)
    ]
    stacked = jnp.concatenate(
        [jnp.concatenate([w[0], w[1]], axis=1), jnp.concatenate([w[1], -w[0]], axis=1)], axis=0
    )
    copies[0].wait()
    for cut in (slice(0, 256), slice(256, 512)):
        y_ref[:, cut] = dot3(stacked, table_ref.at[:, :, cut])
    copies[1].wait()
    copies[2].wait()
    back = 0.0
    for lane_tile in range(4):
        cut = slice(lane_tile * 128, lane_tile * 128 + 128)
        for row in range(4):
            points = []
            for a in range(CELL):
                block = (a % 2) * 4 + a // 2
                value = tuple(tile(y_ref, o, block, row, lane_tile)[...] for o in range(2))
                if a:
                    value = twist(value, twist_ref[a:a + 1, cut], twist_ref[8 + a:9 + a, cut], -1)
                points.append(value)
            spectrum = []
            for q, value in enumerate(dft8(points, -1)):
                first = q * 512 + lane_tile * 128
                green = green_ref[row * 8:row * 8 + 8, first:first + 128]
                spectrum.append((value[0] * green, value[1] * green))
            for a, value in enumerate(dft8(spectrum, 1)):
                block = (a % 2) * 4 + a // 2
                if a:
                    value = twist(value, twist_ref[a:a + 1, cut], twist_ref[8 + a:9 + a, cut], 1)
                for o in range(2):
                    tile(y_ref, o, block, row, lane_tile)[...] = value[o]
        if lane_tile % 2:
            half = slice(lane_tile * 128 - 128, lane_tile * 128 + 128)
            back = back + inverse_cells(y_ref, table_ref, half)
    for c in range(2):
        cells_ref[c, CELLS:] = jnp.zeros((8, 2, 128), F32)
        for h in range(2):
            first = (c * 2 + h) * 128
            cells_ref[c, 0:CELLS, h, :] = back[:, first:first + 128]

    slot = lax.broadcasted_iota(jnp.int32, (SLOTS, 2, 128), 0)

    def scatter(device, start):
        count = counts_ref[device]
        for c in range(2):
            held = cells_ref[c, pl.ds(start, SLOTS)]
            out_ref[device, c] = jnp.where(slot < count, held, 0.0)
        return start + count

    outs = []
    start = 0
    for part in range(4):
        here = slice(part * 32, part * 32 + 32)
        start = lax.fori_loop(part * 32, part * 32 + 32, scatter, start, unroll=8)
        copy = pltpu.make_async_copy(out_ref.at[here], out_hbm.at[here], out_sems.at[part])
        copy.start()
        outs.append(copy)
    for copy in outs:
        copy.wait()


def inverse_cells(y_ref, table_ref, cut):
    re, im = y_ref[0:256, cut], y_ref[256:512, cut]
    by_cos = jnp.concatenate([re, im], axis=0)
    by_sin = jnp.concatenate([-im, re], axis=0)
    return dot3_nt(table_ref[0, 0:256, cut], table_ref[1, 0:256, cut], by_cos) + dot3_nt(
        table_ref[0, 256:512, cut], table_ref[1, 256:512, cut], by_sin
    )


def backward_kernel(
    counts_hbm, x_ref, whole_hbm, part_hbm, above_hbm, below_hbm, couple_hbm, order_hbm,
    table_hbm, twist_hbm, out_hbm,
    counts_ref, part_ref, above_ref, below_ref, couple_ref, first_ref, last_ref, order_ref,
    table_ref, twist_ref, out_ref, y_ref, sems, out_sems,
):
    rest = slice(128, 384)
    first_row = whole_hbm.at[0, :, :, rest]
    copies = fetch(
        (
            twist_hbm, table_hbm, order_hbm, part_hbm,
            above_hbm, below_hbm, couple_hbm, first_row, counts_hbm,
        ),
        (
            twist_ref, table_ref, order_ref, part_ref,
            above_ref, below_ref, couple_ref, first_ref, counts_ref,
        ),
        sems,
    )
    copies.pop().wait()
    count = counts_ref[lax.axis_index("row")]
    copies += fetch(
        (whole_hbm.at[count - 1, :, :, rest],), (last_ref,), sems.at[pl.ds(9, 1)]
    )
    lane = lax.broadcasted_iota(jnp.int32, (64, 128), 1)
    copies[0].wait()
    copies[1].wait()
    back = 0.0
    for lane_tile in range(4):
        cut = slice(lane_tile * 128, lane_tile * 128 + 128)
        for o in range(2):
            tiles = [
                x_ref[:, lane_tile * 4 + u, o * 8:o * 8 + 8, :].reshape(64, 128) for u in range(4)
            ]
            for row, value in enumerate(swap_groups(tiles, lane)):
                for k in range(CELL):
                    tile(y_ref, o, k, row, lane_tile)[...] = value[k * 8:k * 8 + 8, :]
        for row in range(4):
            points = [
                tuple(tile(y_ref, o, k, row, lane_tile)[...] for o in range(2))
                for k in range(CELL)
            ]
            for b, value in enumerate(dft8(points, 1)):
                if b:
                    value = twist(value, twist_ref[b:b + 1, cut], twist_ref[8 + b:9 + b, cut], 1)
                for o in range(2):
                    tile(y_ref, o, b, row, lane_tile)[...] = value[o]
        if lane_tile % 2:
            half = slice(lane_tile * 128 - 128, lane_tile * 128 + 128)
            back = back + inverse_cells(y_ref, table_ref, half)
    copies[2].wait()
    for copy in copies[3:]:
        copy.wait()
    alone = count == 1
    couple = couple_ref[:, rest]
    last_ref[...] = last_ref[...] - couple * (
        below_ref[0, :, :, rest] + jnp.where(alone, above_ref[0, :, :, rest], 0.0)
    )
    last_copy = pltpu.make_async_copy(
        last_ref, out_hbm.at[count - 1, :, :, rest], out_sems.at[SLOTS]
    )
    last_copy.start()
    first_ref[...] = first_ref[...] - couple * (
        above_ref[0, :, :, rest] + jnp.where(alone, below_ref[0, :, :, rest], 0.0)
    )
    near = couple_ref[0:1, 0:128]
    halves = [split(back[:, c * 256:c * 256 + 256]) for c in range(2)]
    outs = []
    for slot in range(SLOTS):
        order = order_ref[:, slot * 128:slot * 128 + 128]
        for c in range(2):
            plane = dot(halves[c][0], order) + dot(halves[c][1], order)
            beside = jnp.where(slot == count - 1, below_ref[0, :, c, 0:128], 0.0)
            if slot == 0:
                beside = beside + above_ref[0, :, c, 0:128]
            out_ref[slot, :, c, :] = part_ref[slot, c] + plane - near * beside
        copy = pltpu.make_async_copy(
            out_ref.at[slot], out_hbm.at[slot, :, :, 0:128], out_sems.at[slot]
        )
        copy.start()
        outs.append(copy)
        if slot == 1:
            last_copy.wait()
            copy = pltpu.make_async_copy(
                first_ref, out_hbm.at[0, :, :, rest], out_sems.at[SLOTS + 1]
            )
            copy.start()
            outs.append(copy)
    for copy in outs:
        copy.wait()


def structural_kernel(
    counts_ref, x_hbm, stiff_hbm, couple_ref, soft_ref, mask_ref, out_hbm, part_hbm,
    x_ref, stiff_ref, plane_ref, part_ref, sems, out_sems,
):
    count = counts_ref[lax.axis_index("row")]
    copies = fetch(
        [stiff_hbm] + [x_hbm.at[slot] for slot in range(SLOTS)],
        [stiff_ref] + [x_ref.at[slot] for slot in range(SLOTS)],
        sems,
    )
    for slot in range(SLOTS):
        copies[1 + slot].wait()
        for c in range(2):
            plane_ref[slot + 1, c] = x_ref[slot, :, c, :]
    copies[0].wait()
    for c in range(2):
        plane_ref[0, c] = jnp.zeros((CELLS, 384), F32)
        plane_ref[count + 1, c] = jnp.zeros((CELLS, 384), F32)
    outs = []
    cell = lax.broadcasted_iota(jnp.int32, (CELLS, 1), 0)
    for slot in range(SLOTS):
        biased = mask_ref[:, slot:slot + 1]
        for c in range(2):
            own = plane_ref[slot + 1, c]
            elastic = dot(own.astype(BF16), stiff_ref[...])
            left = jnp.where(cell == 0, 0.0, pltpu.roll(own, 1, 0))
            right = jnp.where(cell == CELLS - 1, 0.0, pltpu.roll(own, CELLS - 1, 0))
            beside = plane_ref[slot, c] + plane_ref[slot + 2, c] + left + right
            value = elastic - couple_ref[...] * beside - (biased * soft_ref[...]) * own
            value = jnp.where(slot < count, value, 0.0)
            part_ref[slot, c] = value[:, 0:128]
            x_ref[slot, :, c, :] = value
        copy = pltpu.make_async_copy(x_ref.at[slot], out_hbm.at[slot], out_sems.at[slot])
        copy.start()
        outs.append(copy)
    copy = pltpu.make_async_copy(part_ref, part_hbm, out_sems.at[SLOTS])
    copy.start()
    outs.append(copy)
    for copy in outs:
        copy.wait()


HBM = pl.BlockSpec(memory_space=pltpu.HBM)
SCALARS = pl.BlockSpec(memory_space=pltpu.SMEM)
VECTORS = pl.BlockSpec(memory_space=pltpu.VMEM)
CHUNK = (DEVICES, 16, 128)
COUNTS = pltpu.SMEM((DEVICES,), jnp.int32)
ORDER = pltpu.VMEM((256, 512), BF16)
TABLE = pltpu.VMEM((2, 512, 512), BF16)
TURNS = pltpu.VMEM((16, 512), F32)
SPECTRAL = pltpu.VMEM((512, 512), F32)
BLOCK = (SLOTS, CELLS, 2, 384)
EDGE = (1, CELLS, 2, 384)
PARAMS = pltpu.CompilerParams(vmem_limit_bytes=VMEM_LIMIT)


def dma(count):
    return pltpu.SemaphoreType.DMA((count,))


def cost(flops, size):
    return pl.CostEstimate(flops=flops, bytes_accessed=size, transcendentals=0)


def forward(displacement, row_counts, table, turns):
    shape = (8, 16, 16, 128)
    sent, first, last = pl.pallas_call(
        forward_kernel,
        in_specs=[HBM] * 5,
        out_specs=[HBM] * 3,
        out_shape=[
            jax.ShapeDtypeStruct(shape, F32),
            jax.ShapeDtypeStruct(EDGE, F32),
            jax.ShapeDtypeStruct(EDGE, F32),
        ],
        scratch_shapes=[
            COUNTS, pltpu.VMEM((SLOTS, CELLS, 2, 128), F32), ORDER, TABLE, TURNS,
            pltpu.VMEM(shape, F32),
            pltpu.VMEM(EDGE, F32), pltpu.VMEM(EDGE, F32), SPECTRAL, dma(7), dma(6),
        ],
        compiler_params=PARAMS,
        cost_estimate=cost(10**9, 7 << 20),
    )(row_counts, displacement, jnp.asarray(dof_order_table(1.0)), table, turns)
    return sent.reshape(CHUNK), first, last


def middle(received, row_counts, table, turns, green_spectrum):
    shape = (DEVICES, 2, SLOTS, 2, 128)
    sent = pl.pallas_call(
        middle_kernel,
        in_specs=[HBM, VECTORS] + [HBM] * 3,
        out_specs=HBM,
        out_shape=jax.ShapeDtypeStruct(shape, F32),
        scratch_shapes=[
            COUNTS, TABLE, TURNS, pltpu.VMEM((32, PAD), F32),
            pltpu.VMEM(shape, F32), pltpu.VMEM((2, CELLS + 8, 2, 128), F32), SPECTRAL,
            dma(4), dma(4),
        ],
        compiler_params=pltpu.CompilerParams(vmem_limit_bytes=40 * 1024 * 1024),
        cost_estimate=cost(3 * 10**9, 5 << 20),
    )(row_counts, received.reshape(shape), table, turns, green_spectrum)
    return sent.reshape(CHUNK)


def backward(received, structural, part, above, below, coupling, row_counts, table, turns):
    edge = pltpu.VMEM((CELLS, 2, 256), F32)
    return pl.pallas_call(
        backward_kernel,
        in_specs=[HBM, VECTORS] + [HBM] * 8,
        out_specs=HBM,
        out_shape=jax.ShapeDtypeStruct(BLOCK, F32),
        scratch_shapes=[
            COUNTS, pltpu.VMEM((SLOTS, 2, CELLS, 128), F32),
            pltpu.VMEM(EDGE, F32), pltpu.VMEM(EDGE, F32), pltpu.VMEM((2, 384), F32), edge, edge,
            ORDER, TABLE, TURNS, pltpu.VMEM((SLOTS, CELLS, 2, 128), F32), SPECTRAL,
            dma(10), dma(SLOTS + 2),
        ],
        input_output_aliases={2: 0},
        compiler_params=pltpu.CompilerParams(vmem_limit_bytes=40 * 1024 * 1024),
        cost_estimate=cost(10**9, 8 << 20),
    )(
        row_counts, received.reshape(8, 16, 16, 128), structural, part, above, below, coupling,
        jnp.asarray(dof_order_table(1.0 / (PAD * PAD))), table, turns,
    )


def structure(displacement, stiffness, coupling, softening, biased, row_counts):
    return pl.pallas_call(
        structural_kernel,
        in_specs=[SCALARS] + [HBM] * 2 + [VECTORS] * 3,
        out_specs=[HBM] * 2,
        out_shape=[
            jax.ShapeDtypeStruct(BLOCK, F32),
            jax.ShapeDtypeStruct((SLOTS, 2, CELLS, 128), F32),
        ],
        scratch_shapes=[
            pltpu.VMEM(BLOCK, F32), pltpu.VMEM((384, 384), BF16),
            pltpu.VMEM((SLOTS + 2, 2, CELLS, 384), F32),
            pltpu.VMEM((SLOTS, 2, CELLS, 128), F32), dma(5), dma(5),
        ],
        compiler_params=PARAMS,
        cost_estimate=cost(10**9, 8 << 20),
    )(row_counts, displacement, stiffness, coupling, softening, biased)


def per_device(
    displacement, stiffness, coupling, softening, electrode_mask, row_counts, green_spectrum
):
    table = jnp.asarray(dft_table())
    turns = jnp.asarray(twiddle_table())
    devices = lax.axis_size("row")
    up = [(i, i + 1) for i in range(devices - 1)]
    down = [(j, i) for i, j in up]
    sent, first, last = forward(displacement, row_counts, table, turns)
    above = lax.ppermute(last, "row", up)
    below = lax.ppermute(first, "row", down)
    received = lax.all_to_all(sent, "row", split_axis=0, concat_axis=0, tiled=True)
    couple = jnp.broadcast_to(coupling[None, :], (2, 384))
    structural, part = structure(
        displacement, stiffness, coupling[None, :], softening[None, :],
        electrode_mask.astype(F32).T, row_counts,
    )
    sent = middle(received, row_counts, table, turns, green_spectrum)
    received = lax.all_to_all(sent, "row", split_axis=0, concat_axis=0, tiled=True)
    return backward(received, structural, part, above, below, couple, row_counts, table, turns)


def solution(mesh):
    placed = (P("row", None, None, None), P(), P(), P(), P("row", None), P(), P("row", None))
    return jax.shard_map(
        per_device,
        mesh=mesh,
        in_specs=placed,
        out_specs=P("row", None, None, None),
        check_vma=False,
    )
```
